512 devices in a mesh: seq: 64 (over y, x, core), head: 8 (over z).
Axes of the slice: x: 4, y: 8, z: 8, core: 2. Of those that a mesh axis runs over, the one named last changes fastest.
Arguments:
- queries: bfloat16 [8192, 4096], P('seq', 'head'), may hold values from -0.71875 to 0.71875
- key_rows: bfloat16 [8192, 4096], P('seq', 'head'), may hold values from -0.71875 to 0.71875
- value_rows: bfloat16 [8192, 4096], P('seq', 'head'), may hold values from -0.71875 to 0.71875
- segment_ids: int32 [8192], P('seq'), may hold values from 0 to 7, never falling along the last dimension, each value on 1 to 2048 neighbouring positions
- decay_span: float32 [32], P('head'), may hold values from 30 to 81920, as said below
- norm_gain: float32 [4096], P('head'), may hold values from 0.5 to 1.5
- out_grad: bfloat16 [8192, 4096], P('seq', 'head'), may hold values from -0.71875 to 0.71875
Outputs:
- query_grad: bfloat16 [8192, 4096], P('seq', 'head')
- key_grad: bfloat16 [8192, 4096], P('seq', 'head')
- value_grad: bfloat16 [8192, 4096], P('seq', 'head')
- gain_grad: float32 [4096], P('head')
The draws below stay inside these ranges and needn't reach their ends.
Inputs may be any that keep to these rules, and one draw needn't show every extreme that they name: segment_ids never falls along the segment; every document of the 8 has a token and the longest has 2048. The decay per token of head h is exp(-1 / decay_span[h]).
All inputs are finite; a program needn't handle non-finite values.
Results may differ from the reference program's by a relative error of at most 0.0012.
Values sent between devices are 32-bit elements; how exact they have to be, the bound alone decides.
A program may use at most 64 MiB of HBM per device.

```python
import math
import jax
import jax.numpy as jnp
import numpy as np
from jax import lax

HEADS = 32
HEAD_DIM = 128
DOCS = 8
TOKENS = 8192
FEATURES = 4096
DOC_MOST = 2048


def draw_decay_span(key, part):
    key_pick, key_fast, key_slow, key_place = jax.random.split(jax.random.fold_in(key, 17), 4)
    fast_share = 0.5
    chooser = jax.random.uniform(key_pick, (HEADS,), jnp.float32)
    fast_span = jax.random.uniform(key_fast, (HEADS,), jnp.float32, 30.0, 50.0)
    low_log = jnp.log(jnp.float32(0.5 * TOKENS))
    high_log = jnp.log(jnp.float32(10.0 * TOKENS))
    slow_span = jnp.exp(jax.random.uniform(key_slow, (HEADS,), jnp.float32, low_log, high_log))
    spans = jnp.where(chooser < fast_share, fast_span, slow_span)
    place = jax.random.randint(key_place, (), 0, HEADS)
    spans = spans.at[place].set(30.0)
    spans = spans.at[(place + 1) % HEADS].set(jnp.float32(10.0 * TOKENS))
    return spans.astype(jnp.float32)


def levels(stream_key, dims, cuts, low, high):
    factor_of, own = 1.0, jax.random.fold_in(stream_key, 6)
    for dim, parts in cuts:
        heights = jnp.exp(jax.random.uniform(jax.random.fold_in(own, dim), (parts,), jnp.float32, low / len(cuts), high / len(cuts)))
        factor_of = factor_of * jnp.repeat(heights, dims[dim] // parts).reshape([-1 if axis == dim else 1 for axis in range(len(dims))])
    return factor_of


def length_profile(number_of, total, bound, skew):
    loads = [(1 << 20) // math.isqrt(rank ** skew) + 1 for rank in range(2, number_of + 1)]
    surplus, holding = total - bound - (number_of - 1), [1] * (number_of - 1)
    while surplus > 0:
        candidates = [i for i in range(number_of - 1) if holding[i] < bound]
        mass, budget = sum([loads[i] for i in candidates]), surplus
        for i in candidates:
            addition = min(bound - holding[i], max(1, budget * loads[i] // mass), surplus)
            holding[i] = holding[i] + addition
            surplus = surplus - addition
    return np.array([bound] + holding)


def ragged_sizes(rng, count, total, limit, skew):
    if count == 2:
        one = jax.random.randint(rng, (), max(1, total - limit), min(limit, total - 1) + 1)
        return jnp.stack([one, total - one])
    tallies = jnp.asarray(length_profile(count, total, limit, skew), jnp.int32)
    couples = (count - 1) // 2
    source_of, taker = tallies[1:1 + 2 * couples:2], tallies[2:2 + 2 * couples:2]
    margin = jnp.minimum(source_of - 1, limit - taker)
    passed = jax.random.randint(jax.random.fold_in(rng, 1), (couples,), 0, 1 << 20) % (margin + 1)
    tallies = tallies.at[1:1 + 2 * couples:2].set(source_of - passed).at[2:2 + 2 * couples:2].set(taker + passed)
    return tallies[jax.random.permutation(jax.random.fold_in(rng, 2), count)]


def normal_values(stream_key, extent, width, most, pieces=(), held_as=jnp.bfloat16):
    values = jax.random.normal(stream_key, extent, jnp.float32) * width
    if len(pieces) > 0:
        values = levels(stream_key, extent, pieces, -0.22, 0.18) * values
    return jnp.clip(values, min=-most, max=most).astype(held_as)


def setup_inputs(seed: int = 0) -> dict:
    splits = jax.random.split(jax.random.key(seed), 8)
    return {
        "queries": normal_values(splits[0], (TOKENS, FEATURES), 0.12, 0.71875, ((0, 64), (1, 8))),
        "key_rows": normal_values(splits[1], (TOKENS, FEATURES), 0.12, 0.71875, ((0, 64), (1, 8))),
        "value_rows": normal_values(splits[2], (TOKENS, FEATURES), 0.12, 0.71875, ((0, 64), (1, 8))),
        "segment_ids": jnp.searchsorted(jnp.cumsum(ragged_sizes(splits[3], DOCS, TOKENS, DOC_MOST, 0)), jnp.arange(TOKENS), side="right").astype(jnp.int32),
        "decay_span": draw_decay_span(jax.random.fold_in(splits[7], 71), 0),
        "norm_gain": jnp.clip(1.0 + 0.1 * jax.random.normal(splits[5], (FEATURES,), jnp.float32), 0.5, 1.5),
        "out_grad": normal_values(splits[6], (TOKENS, FEATURES), 0.12, 0.71875, ((0, 64), (1, 8))),
    }


exact = lax.Precision.HIGHEST

def reference(queries, key_rows, value_rows, segment_ids, decay_span, norm_gain, out_grad):
    group_rows = 128
    group_count = TOKENS // group_rows
    all_features = HEADS * HEAD_DIM
    spans = decay_span.astype(jnp.float32)
    gain_vec = norm_gain.astype(jnp.float32)
    offsets = jnp.arange(group_rows).astype(jnp.float32)
    offset_gap = offsets[:, None] - offsets[None, :]
    causal = offset_gap >= 0
    decay_tile = jnp.where(causal[None], jnp.exp(-jnp.maximum(offset_gap, 0.0)[None] / spans[:, None, None]), 0.0)
    into_weight = jnp.exp(-(offsets + 1.0)[:, None] / spans[None, :])
    tail_weight = jnp.exp(-(group_rows - 1.0 - offsets)[:, None] / spans[None, :])
    start_weight = jnp.exp(-offsets[:, None] / spans[None, :])
    next_weight = jnp.exp(-(group_rows - offsets)[:, None] / spans[None, :])
    whole_weight = jnp.exp(-group_rows / spans)

    def split_heads(array):
        return array.reshape(group_count, group_rows, HEADS, HEAD_DIM)
    query_blocks = split_heads(queries)
    key_blocks = split_heads(key_rows)
    value_blocks = split_heads(value_rows)
    grad_blocks = out_grad.reshape(group_count, group_rows, all_features)
    seg_blocks = segment_ids.astype(jnp.float32).reshape(group_count, group_rows)

    def forward_step(carry, inputs):
        state_now, carry_seg = carry
        query_blk, key_blk, value_blk, dy_blk, seg_blk = inputs
        query_blk = query_blk.astype(jnp.float32)
        key_blk = key_blk.astype(jnp.float32)
        value_blk = value_blk.astype(jnp.float32)
        dy_full = dy_blk.astype(jnp.float32)
        same_doc = (seg_blk[:, None] == seg_blk[None, :]).astype(jnp.float32)
        weights = decay_tile * same_doc[None]
        scores = jnp.einsum('thd,shd->hts', query_blk, key_blk, precision=exact) * weights
        inter_on = jnp.where((seg_blk == carry_seg)[:, None], into_weight, 0.0)
        attended = jnp.einsum('hts,shd->thd', scores, value_blk, precision=exact)
        attended = attended + inter_on[:, :, None] * jnp.einsum('thi,hij->thj', query_blk, state_now, precision=exact)
        flat_out = attended.reshape(group_rows, all_features)
        inv_scale = lax.rsqrt(lax.optimization_barrier(jnp.sum(flat_out * flat_out, axis=1)) / all_features + 1e-06)
        cross = lax.optimization_barrier(jnp.sum(dy_full * gain_vec[None, :] * flat_out, axis=1))
        out_back = gain_vec[None, :] * dy_full * inv_scale[:, None] - flat_out * (inv_scale * inv_scale * inv_scale * cross / all_features)[:, None]
        gain_part = lax.optimization_barrier(jnp.sum(dy_full * flat_out * inv_scale[:, None], axis=0))
        back_heads = out_back.reshape(group_rows, HEADS, HEAD_DIM)
        grad_scores = jnp.einsum('thd,shd->hts', back_heads, value_blk, precision=exact) * weights
        query_part = jnp.einsum('hts,shd->thd', grad_scores, key_blk, precision=exact)
        query_part = query_part + inter_on[:, :, None] * jnp.einsum('thj,hij->thi', back_heads, state_now, precision=exact)
        tail_on = jnp.where((seg_blk == seg_blk[-1])[:, None], tail_weight, 0.0)
        passes = jnp.logical_and(seg_blk[0] == seg_blk[-1], seg_blk[0] == carry_seg)
        factor = jnp.where(passes, whole_weight, 0.0)
        new_state = jnp.einsum('thi,thj->hij', key_blk * tail_on[:, :, None], value_blk, precision=exact) + factor[:, None, None] * state_now
        return ((new_state, seg_blk[-1]), (back_heads, query_part.reshape(group_rows, all_features).astype(jnp.bfloat16), gain_part))
    start_carry = (jnp.zeros((HEADS, HEAD_DIM, HEAD_DIM), jnp.float32), jnp.float32(-1.0))
    _, (back_blocks, query_grad, gain_parts) = lax.scan(forward_step, start_carry, (query_blocks, key_blocks, value_blocks, grad_blocks, seg_blocks))

    def backward_step(carry, inputs):
        grad_state, carry_seg = carry
        query_blk, key_blk, value_blk, back_heads, seg_blk = inputs
        query_blk = query_blk.astype(jnp.float32)
        key_blk = key_blk.astype(jnp.float32)
        value_blk = value_blk.astype(jnp.float32)
        same_doc = (seg_blk[:, None] == seg_blk[None, :]).astype(jnp.float32)
        weights = decay_tile * same_doc[None]
        scores = jnp.einsum('thd,shd->hts', query_blk, key_blk, precision=exact) * weights
        grad_scores = jnp.einsum('thd,shd->hts', back_heads, value_blk, precision=exact) * weights
        back_on = jnp.where((seg_blk == carry_seg)[:, None], next_weight, 0.0)
        key_part = jnp.einsum('hts,thd->shd', grad_scores, query_blk, precision=exact)
        key_part = key_part + back_on[:, :, None] * jnp.einsum('hij,shj->shi', grad_state, value_blk, precision=exact)
        value_part = jnp.einsum('hts,thd->shd', scores, back_heads, precision=exact)
        value_part = value_part + back_on[:, :, None] * jnp.einsum('hij,shi->shj', grad_state, key_blk, precision=exact)
        start_on = jnp.where((seg_blk == seg_blk[0])[:, None], start_weight, 0.0)
        passes = jnp.logical_and(seg_blk[0] == seg_blk[-1], seg_blk[-1] == carry_seg)
        factor = jnp.where(passes, whole_weight, 0.0)
        new_state = jnp.einsum('thi,thj->hij', query_blk * start_on[:, :, None], back_heads, precision=exact) + factor[:, None, None] * grad_state
        return ((new_state, seg_blk[0]), (key_part.reshape(group_rows, all_features).astype(jnp.bfloat16), value_part.reshape(group_rows, all_features).astype(jnp.bfloat16)))
    _, (key_grad, value_grad) = lax.scan(backward_step, start_carry, (query_blocks, key_blocks, value_blocks, back_blocks, seg_blocks), reverse=True)
    gain_grad = lax.optimization_barrier(jnp.sum(gain_parts, axis=0))
    return (query_grad.reshape(TOKENS, all_features), key_grad.reshape(TOKENS, all_features), value_grad.reshape(TOKENS, all_features), gain_grad)
```

```python
import functools

import jax
import jax.numpy as jnp
from jax import lax
from jax.experimental import pallas as pl
from jax.experimental.pallas import tpu as pltpu
from jax.sharding import PartitionSpec as P

DIM = 128
ROW = 8
BLOCK = 128
HALF = 64
MESH = pl.DeviceIdType.MESH
F32 = jnp.float32
BF16 = jnp.bfloat16
ORDER = (4, 3, 5, 2, 6, 1, 7)


def split(x):
    high = x.astype(BF16)
    return high, (x - high.astype(F32)).astype(BF16)


def mm(a, b, ca, cb):
    return lax.dot_general(a, b, (((ca,), (cb,)), ((), ())), preferred_element_type=F32)


def mm_split_left(a, b, ca, cb):
    return mm(a[0], b, ca, cb) + mm(a[1], b, ca, cb)


def mm_split_right(a, b, ca, cb):
    return mm(a, b[0], ca, cb) + mm(a, b[1], ca, cb)


def mm_split_both(a, b, ca, cb):
    return mm(a[0], b[0], ca, cb) + (mm(a[0], b[1], ca, cb) + mm(a[1], b[0], ca, cb))


def kernel(
    rows, zs, heads,
    q_hbm, k_hbm, v_hbm, dy_hbm, seg_ref, span_ref, gain_ref,
    dq_ref, dk_ref, dv_ref, gg_ref,
    q_ref, k_ref, v_ref, dy_ref,
    meta_own, meta, states, gathered, totals, carried, prefixes, state_in,
    z_own, z_all, gr_own, gr_all, gc_own, gc_all,
    att_ref, back_ref, w_ref, dk_acc, dv_acc, qk_ref,
    in_sem, meta_s, meta_r, a2a_s, a2a_r, col_s, col_r, ret_s, ret_r,
    z_s, z_r, gr_s, gr_r, gc_s, gc_r,
):
    me = lax.axis_index("seq")
    z = lax.axis_index("head")
    row = me // ROW
    pos = lax.rem(me, ROW)
    features = float(zs * heads * DIM)

    loads = [
        pltpu.make_async_copy(src, dst, in_sem.at[i])
        for i, (src, dst) in enumerate(
            ((k_hbm, k_ref), (v_hbm, v_ref), (q_hbm, q_ref), (dy_hbm, dy_ref))
        )
    ]
    for copy in loads:
        copy.start()

    def seq_of(r, p):
        return {"seq": r * ROW + p, "head": z}

    row_mates = [lax.rem(pos + s, ROW) for s in ORDER]
    col_mates = [lax.rem(row + s, rows) for s in range(1, rows)]
    z_mates = [lax.rem(z + s, zs) for s in range(1, zs)]
    barrier = pltpu.get_barrier_semaphore()
    for p in row_mates:
        pl.semaphore_signal(barrier, inc=1, device_id=seq_of(row, p), device_id_type=MESH)
    for r in col_mates:
        pl.semaphore_signal(barrier, inc=1, device_id=seq_of(r, pos), device_id_type=MESH)
    for other in z_mates:
        pl.semaphore_signal(
            barrier, inc=1, device_id={"seq": me, "head": other}, device_id_type=MESH
        )

    def remote(src, dst, ss, rs, target):
        return pltpu.make_async_remote_copy(
            src_ref=src, dst_ref=dst, send_sem=ss, recv_sem=rs,
            device_id=target, device_id_type=MESH,
        )

    pending = []

    def send(*args):
        copy = remote(*args)
        copy.start()
        pending.append(copy)

    def arrived(buffer, ss, rs):
        remote(buffer, buffer, ss, rs, seq_of(row, row_mates[0])).wait_recv()

    t_col = lax.broadcasted_iota(jnp.int32, (BLOCK, DIM), 0).astype(F32)
    s_row = lax.broadcasted_iota(jnp.int32, (BLOCK, DIM), 1).astype(F32)
    seg_row = seg_ref[...].astype(F32)
    seg_tile = jnp.broadcast_to(seg_row, (BLOCK, DIM))
    seg_col = seg_tile.T
    first_own = jnp.broadcast_to(seg_row[:, 0:1], (1, DIM))
    last_own = jnp.broadcast_to(seg_row[:, BLOCK - 1:BLOCK], (1, DIM))
    tile_row = lax.broadcasted_iota(jnp.int32, (8, DIM), 0)
    meta_own[...] = jnp.where(tile_row == 0, last_own, first_own)
    meta[pos] = meta_own[...]

    inverse = [1.0 / jnp.full((1, DIM), span_ref[h], F32) for h in range(heads)]
    own_inverse = 1.0 / jnp.full((1, DIM), span_ref[pos // 2], F32)
    lam = jnp.exp(-float(BLOCK) * own_inverse)
    lam_row = jnp.exp(-float(BLOCK * ROW) * own_inverse)

    loads[0].wait()
    loads[1].wait()
    for h in range(heads):
        cut = slice(h * DIM, (h + 1) * DIM)
        tail = jnp.where(seg_col == last_own, jnp.exp((t_col - (BLOCK - 1.0)) * inverse[h]), 0.0)
        local = mm_split_right(
            k_ref[:, cut], split(v_ref[:, cut].astype(F32) * tail), 0, 0
        )
        states[0, 2 * h] = local[:HALF]
        states[0, 2 * h + 1] = local[HALF:]

    pl.semaphore_wait(barrier, len(row_mates) + len(col_mates) + len(z_mates))

    def scatter(side):
        for i, p in enumerate(row_mates):
            send(
                states.at[side, p], gathered.at[side, pos],
                a2a_s.at[side, i], a2a_r.at[side, pos], seq_of(row, p),
            )
        gathered[side, pos] = states[side, pos]

    for i, p in enumerate(row_mates):
        send(meta_own, meta.at[pos], meta_s.at[i], meta_r.at[pos], seq_of(row, p))
    scatter(0)

    def scan_first(side):
        for i, p in enumerate(row_mates):
            arrived(gathered.at[side, p], a2a_s.at[side, i], a2a_r.at[side, p])
        order = list(range(ROW)) if side == 0 else list(range(ROW - 1, -1, -1))
        seg_of = [meta[a, side:side + 1, :] for a in order]
        run = gathered[side, order[0]]
        for n in range(1, ROW):
            run = gathered[side, order[n]] + jnp.where(seg_of[n] == seg_of[n - 1], lam, 0.0) * run
        totals[side, :HALF] = run
        totals[side, HALF:] = jnp.broadcast_to(seg_of[-1], (8, DIM))
        for step in range(2):
            move = step + 1 if side == 0 else rows - step - 1
            send(
                totals.at[side], carried.at[side, step],
                col_s.at[side, step], col_r.at[side, step],
                seq_of(lax.rem(row + move, rows), pos),
            )

    def scan_second(side):
        for step in range(2):
            arrived(carried.at[side, step], col_s.at[side, step], col_r.at[side, step])
        order = list(range(ROW)) if side == 0 else list(range(ROW - 1, -1, -1))
        seg_of = [meta[a, side:side + 1, :] for a in order]
        before = row if side == 0 else rows - 1 - row
        near_seg = carried[side, 0, HALF:HALF + 1]
        far_seg = carried[side, 1, HALF:HALF + 1]
        near_seg = jnp.where(before >= 1, near_seg, -1.0)
        far_on = jnp.where(before >= 2, jnp.where(far_seg == near_seg, lam_row, 0.0), 0.0)
        near_on = jnp.where(before >= 1, 1.0, 0.0)
        run = carried[side, 0, :HALF] * near_on + far_on * carried[side, 1, :HALF]
        prev = near_seg
        for n in range(ROW):
            prefixes[side, order[n]] = run
            if n < ROW - 1:
                run = gathered[side, order[n]] + jnp.where(seg_of[n] == prev, lam, 0.0) * run
                prev = seg_of[n]
        for i, p in enumerate(row_mates):
            send(
                prefixes.at[side, p], state_in.at[side, pos],
                ret_s.at[side, i], ret_r.at[side, pos], seq_of(row, p),
            )
        state_in[side, pos] = prefixes[side, pos]
        return near_seg

    def scan_last(side):
        for i, p in enumerate(row_mates):
            arrived(state_in.at[side, p], ret_s.at[side, i], ret_r.at[side, p])

    loads[2].wait()
    causal = t_col >= s_row
    same = seg_col == seg_tile
    keep = jnp.logical_and(causal, same)
    for h in range(heads):
        cut = slice(h * DIM, (h + 1) * DIM)
        weights = jnp.where(keep, jnp.exp(jnp.minimum(s_row - t_col, 0.0) * inverse[h]), 0.0)
        w_ref[h] = weights
        scores = split(mm(q_ref[:, cut], k_ref[:, cut], 1, 1) * weights)
        qk_ref[h, 0] = scores[0]
        qk_ref[h, 1] = scores[1]
        att_ref[h] = mm_split_left(scores, v_ref[:, cut], 1, 0)

    for i, p in enumerate(row_mates):
        arrived(meta.at[p], meta_s.at[i], meta_r.at[p])
    scan_first(0)
    prev_row_seg = scan_second(0)
    prev_seg = jnp.where(pos == 0, prev_row_seg, meta[lax.rem(pos + ROW - 1, ROW), 0:1, :])
    loads[3].wait()
    scan_last(0)

    into_on = seg_col == prev_seg
    squares = jnp.zeros((BLOCK, DIM), F32)
    crosses = jnp.zeros((BLOCK, DIM), F32)
    for h in range(heads):
        cut = slice(h * DIM, (h + 1) * DIM)
        into = jnp.where(into_on, jnp.exp(-(t_col + 1.0) * inverse[h]), 0.0)
        state = split(state_in[0, 2 * h:2 * h + 2].reshape(DIM, DIM))
        att = att_ref[h] + into * mm_split_right(q_ref[:, cut], state, 1, 0)
        att_ref[h] = att
        squares = squares + att * att
        crosses = crosses + dy_ref[:, cut].astype(F32) * gain_ref[:, cut] * att
    square_row = jnp.sum(squares.T, axis=0, keepdims=True)
    cross_row = jnp.sum(crosses.T, axis=0, keepdims=True)
    z_own[...] = jnp.where(tile_row == 0, square_row, cross_row)
    for i, other in enumerate(z_mates):
        send(z_own, z_all.at[z], z_s.at[i], z_r.at[z], {"seq": me, "head": other})
    z_all[z] = z_own[...]
    for i, other in enumerate(z_mates):
        arrived(z_all.at[other], z_s.at[i], z_r.at[other])
    both = z_all[0]
    for i in range(1, zs):
        both = both + z_all[i]
    inv_row = lax.rsqrt(both[0:1] / features + 1e-06)
    off_row = inv_row * inv_row * inv_row * both[1:2] / features
    inv = jnp.broadcast_to(inv_row, (BLOCK, DIM)).T
    off = jnp.broadcast_to(off_row, (BLOCK, DIM)).T

    for h in range(heads):
        cut = slice(h * DIM, (h + 1) * DIM)
        dy = dy_ref[:, cut].astype(F32)
        att = att_ref[h]
        scaled = dy * inv
        back = gain_ref[:, cut] * scaled - att * off
        back_ref[h] = back
        gr_own[h:h + 1] = jnp.sum(scaled * att, axis=0, keepdims=True)
        start = jnp.where(seg_col == first_own, jnp.exp(-t_col * inverse[h]), 0.0)
        local = mm_split_right(q_ref[:, cut], split(back * start), 0, 0)
        states[1, 2 * h] = local[:HALF]
        states[1, 2 * h + 1] = local[HALF:]
    scatter(1)
    for i, p in enumerate(row_mates):
        send(gr_own, gr_all.at[pos], gr_s.at[i], gr_r.at[pos], seq_of(row, p))
    gr_all[pos] = gr_own[...]

    def inner(h):
        cut = slice(h * DIM, (h + 1) * DIM)
        back = split(back_ref[h])
        weights = w_ref[h]
        grads = split(mm_split_left(back, v_ref[:, cut], 1, 1) * weights)
        into = jnp.where(into_on, jnp.exp(-(t_col + 1.0) * inverse[h]), 0.0)
        state = split(state_in[0, 2 * h:2 * h + 2].reshape(DIM, DIM))
        dq = mm_split_left(grads, k_ref[:, cut], 1, 0) + into * mm_split_both(back, state, 1, 1)
        dq_ref[:, cut] = dq.astype(BF16)
        dk_acc[h] = mm_split_left(grads, q_ref[:, cut], 0, 0)
        dv_acc[h] = mm_split_both((qk_ref[h, 0], qk_ref[h, 1]), back, 0, 0)

    inner(0)
    inner(1)
    scan_first(1)
    for i, p in enumerate(row_mates):
        arrived(gr_all.at[p], gr_s.at[i], gr_r.at[p])
    total = gr_all[0]
    for a in range(1, ROW):
        total = total + gr_all[a]
    gc_own[...] = total
    gc_all[row] = total
    for i, r in enumerate(col_mates):
        send(gc_own, gc_all.at[row], gc_s.at[i], gc_r.at[row], seq_of(r, pos))
    inner(2)
    next_row_seg = scan_second(1)
    next_seg = jnp.where(pos == ROW - 1, next_row_seg, meta[lax.rem(pos + 1, ROW), 1:2, :])
    inner(3)
    for i, r in enumerate(col_mates):
        arrived(gc_all.at[r], gc_s.at[i], gc_r.at[r])
    total = gc_all[0]
    for a in range(1, rows):
        total = total + gc_all[a]
    for h in range(heads):
        gg_ref[:, h * DIM:(h + 1) * DIM] = total[h:h + 1]
    scan_last(1)

    next_on = seg_col == next_seg
    for h in range(heads):
        cut = slice(h * DIM, (h + 1) * DIM)
        weight = jnp.where(next_on, jnp.exp((t_col - float(BLOCK)) * inverse[h]), 0.0)
        grad = split(state_in[1, 2 * h:2 * h + 2].reshape(DIM, DIM))
        dk = dk_acc[h] + weight * mm_split_right(v_ref[:, cut], grad, 1, 1)
        dv = dv_acc[h] + weight * mm_split_right(k_ref[:, cut], grad, 1, 0)
        dk_ref[:, cut] = dk.astype(BF16)
        dv_ref[:, cut] = dv.astype(BF16)
    for copy in pending:
        copy.wait_send()


def local(queries, key_rows, value_rows, segment_ids, decay_span, norm_gain, out_grad):
    rows = lax.axis_size("seq") // ROW
    zs = lax.axis_size("head")
    heads = decay_span.shape[0]
    width = heads * DIM
    whole = pl.BlockSpec(memory_space=pltpu.VMEM)
    far = pl.BlockSpec(memory_space=pl.ANY)
    wide = pltpu.VMEM((BLOCK, width), BF16)
    square = pltpu.VMEM((heads, DIM, DIM), F32)
    dma = pltpu.SemaphoreType.DMA
    out = jax.ShapeDtypeStruct((BLOCK, width), BF16)
    dq, dk, dv, gg = pl.pallas_call(
        functools.partial(kernel, rows, zs, heads),
        out_shape=(out, out, out, jax.ShapeDtypeStruct((1, width), F32)),
        in_specs=[far] * 4 + [whole, pl.BlockSpec(memory_space=pltpu.SMEM), whole],
        out_specs=(whole,) * 4,
        scratch_shapes=[
            wide, wide, wide, wide,
            pltpu.VMEM((8, DIM), F32),
            pltpu.VMEM((ROW, 8, DIM), F32),
            pltpu.VMEM((2, ROW, HALF, DIM), F32),
            pltpu.VMEM((2, ROW, HALF, DIM), F32),
            pltpu.VMEM((2, HALF + 8, DIM), F32),
            pltpu.VMEM((2, 2, HALF + 8, DIM), F32),
            pltpu.VMEM((2, ROW, HALF, DIM), F32),
            pltpu.VMEM((2, ROW, HALF, DIM), F32),
            pltpu.VMEM((8, DIM), F32),
            pltpu.VMEM((zs, 8, DIM), F32),
            pltpu.VMEM((heads, DIM), F32),
            pltpu.VMEM((ROW, heads, DIM), F32),
            pltpu.VMEM((heads, DIM), F32),
            pltpu.VMEM((rows, heads, DIM), F32),
            square, square, square, square, square,
            pltpu.VMEM((heads, 2, DIM, DIM), BF16),
            dma((4,)),
            dma((ROW,)), dma((ROW,)),
            dma((2, ROW)), dma((2, ROW)),
            dma((2, 2)), dma((2, 2)),
            dma((2, ROW)), dma((2, ROW)),
            dma((zs,)), dma((zs,)),
            dma((ROW,)), dma((ROW,)),
            dma((rows,)), dma((rows,)),
        ],
        compiler_params=pltpu.CompilerParams(collective_id=0, has_side_effects=True),
    )(
        queries, key_rows, value_rows, out_grad,
        segment_ids.reshape(1, BLOCK), decay_span, norm_gain.reshape(1, width),
    )
    return dq, dk, dv, gg.reshape(width)


def solution(mesh):
    in_specs = (
        P("seq", "head"),
        P("seq", "head"),
        P("seq", "head"),
        P("seq"),
        P("head"),
        P("head"),
        P("seq", "head"),
    )
    out_specs = (P("seq", "head"), P("seq", "head"), P("seq", "head"), P("head"))
    return jax.shard_map(local, mesh=mesh, in_specs=in_specs, out_specs=out_specs, check_vma=False)
```

```python
import functools

import jax
import jax.numpy as jnp
from jax import lax
from jax.experimental import pallas as pl
from jax.experimental.pallas import tpu as pltpu
from jax.sharding import PartitionSpec as P

DIM = 128
ROW = 8
BLOCK = 128
HALF = 64
CHUNKS = 4
PART = HALF // CHUNKS
HEAD_ROWS = 8
MESH = pl.DeviceIdType.MESH
F32 = jnp.float32
BF16 = jnp.bfloat16
ORDER = (4, 3, 5, 2, 6, 1, 7)


def split(x):
    high = x.astype(BF16)
    return high, (x - high.astype(F32)).astype(BF16)


def mm(a, b, ca, cb):
    return lax.dot_general(a, b, (((ca,), (cb,)), ((), ())), preferred_element_type=F32)


def mm_split_left(a, b, ca, cb):
    return mm(a[0], b, ca, cb) + mm(a[1], b, ca, cb)


def mm_split_right(a, b, ca, cb):
    return mm(a, b[0], ca, cb) + mm(a, b[1], ca, cb)


def mm_split_both(a, b, ca, cb):
    return mm(a[0], b[0], ca, cb) + (mm(a[0], b[1], ca, cb) + mm(a[1], b[0], ca, cb))


def kernel(
    rows, zs, heads,
    q_hbm, k_hbm, v_hbm, dy_hbm, seg_hbm, span_hbm, gain_hbm,
    dq_ref, dk_ref, dv_ref, gg_ref,
    q_ref, k_ref, v_ref, dy_ref, seg_ref, span_ref, gain_ref,
    meta_own, meta, states, gathered, totals, carried, prefixes, state_in,
    z_own, z_all, gr_own, gr_all, gc_own, gc_all,
    att_ref, back_ref, w_ref, dk_acc, dv_acc, qk_ref,
    in_sem, meta_s, meta_r, a2a_s, a2a_r, col_s, col_r, ret_s, ret_r,
    z_s, z_r, gr_s, gr_r, gc_s, gc_r,
):
    me = lax.axis_index("seq")
    z = lax.axis_index("head")
    row = me // ROW
    pos = lax.rem(me, ROW)
    features = float(zs * heads * DIM)

    loads = [
        pltpu.make_async_copy(src, dst, in_sem.at[i])
        for i, (src, dst) in enumerate(
            (
                (k_hbm, k_ref), (v_hbm, v_ref), (q_hbm, q_ref), (dy_hbm, dy_ref),
                (seg_hbm, seg_ref), (span_hbm, span_ref), (gain_hbm, gain_ref),
            )
        )
    ]
    for i in (4, 5, 0, 1, 2, 3, 6):
        loads[i].start()

    def seq_of(r, p):
        return {"seq": r * ROW + p, "head": z}

    row_mates = [lax.rem(pos + s, ROW) for s in ORDER]
    col_mates = [lax.rem(row + s, rows) for s in range(1, rows)]
    z_mates = [lax.rem(z + s, zs) for s in sorted(range(1, zs), key=lambda s: -min(s, zs - s))]
    barrier = pltpu.get_barrier_semaphore()
    for p in row_mates:
        pl.semaphore_signal(barrier, inc=1, device_id=seq_of(row, p), device_id_type=MESH)
    for r in col_mates:
        pl.semaphore_signal(barrier, inc=1, device_id=seq_of(r, pos), device_id_type=MESH)
    for other in z_mates:
        pl.semaphore_signal(
            barrier, inc=1, device_id={"seq": me, "head": other}, device_id_type=MESH
        )

    def remote(src, dst, ss, rs, target):
        return pltpu.make_async_remote_copy(
            src_ref=src, dst_ref=dst, send_sem=ss, recv_sem=rs,
            device_id=target, device_id_type=MESH,
        )

    def send(*args):
        remote(*args).start()

    def arrived(buffer, rs):
        remote(buffer, buffer, rs, rs, seq_of(row, row_mates[0])).wait_recv()

    def sent(buffer, ss):
        remote(buffer, buffer, ss, ss, seq_of(row, row_mates[0])).wait_send()

    row_others = pl.ds(0, ROW - 1)
    loads[4].wait()
    loads[5].wait()

    t_col = lax.broadcasted_iota(jnp.int32, (BLOCK, DIM), 0).astype(F32)
    s_row = lax.broadcasted_iota(jnp.int32, (BLOCK, DIM), 1).astype(F32)
    seg_row = seg_ref[...].astype(F32)
    seg_tile = jnp.broadcast_to(seg_row, (BLOCK, DIM))
    seg_col = seg_tile.T
    first_own = jnp.broadcast_to(seg_row[:, 0:1], (1, DIM))
    last_own = jnp.broadcast_to(seg_row[:, BLOCK - 1:BLOCK], (1, DIM))
    tile_row = lax.broadcasted_iota(jnp.int32, (8, DIM), 0)
    meta_own[...] = jnp.where(tile_row == 0, last_own, first_own)
    meta[pos] = meta_own[...]

    inverse = [1.0 / jnp.full((1, DIM), span_ref[h], F32) for h in range(heads)]
    own_inverse = 1.0 / jnp.full((1, DIM), span_ref[pos // 2], F32)
    lam = jnp.exp(-float(BLOCK) * own_inverse)
    lam_row = jnp.exp(-float(BLOCK * ROW) * own_inverse)

    loads[0].wait()
    loads[1].wait()
    for h in range(heads):
        cut = slice(h * DIM, (h + 1) * DIM)
        tail = jnp.where(seg_col == last_own, jnp.exp((t_col - (BLOCK - 1.0)) * inverse[h]), 0.0)
        local = mm_split_right(
            k_ref[:, cut], split(v_ref[:, cut].astype(F32) * tail), 0, 0
        )
        states[0, 2 * h] = local[:HALF]
        states[0, 2 * h + 1] = local[HALF:]

    pl.semaphore_wait(barrier, len(row_mates) + len(col_mates) + len(z_mates))

    def scatter(side):
        for c in range(CHUNKS):
            part = pl.ds(c * PART, PART)
            for p in row_mates:
                send(
                    states.at[side, p, part], gathered.at[side, pos, part],
                    a2a_s.at[side], a2a_r.at[side, c], seq_of(row, p),
                )
        gathered[side, pos] = states[side, pos]

    def piece(c):
        return pl.ds(HEAD_ROWS + c * PART, PART) if c else pl.ds(0, HEAD_ROWS + PART)

    def order_of(side):
        order = list(range(ROW)) if side == 0 else list(range(ROW - 1, -1, -1))
        return order, [meta[a, side:side + 1, :] for a in order]

    for p in row_mates:
        send(meta_own, meta.at[pos], meta_s.at[0], meta_r.at[0], seq_of(row, p))
    scatter(0)

    def scan_first(side):
        order, seg_of = order_of(side)
        factor = [jnp.where(seg_of[n] == seg_of[n - 1], lam, 0.0) for n in range(1, ROW)]
        for c in range(CHUNKS):
            part = pl.ds(c * PART, PART)
            arrived(gathered.at[side, row_others, part], a2a_r.at[side, c])
            run = gathered[side, order[0], part]
            for n in range(1, ROW):
                run = gathered[side, order[n], part] + factor[n - 1] * run
            if c == 0:
                totals[side, :HEAD_ROWS] = jnp.broadcast_to(seg_of[-1], (HEAD_ROWS, DIM))
            totals[side, pl.ds(HEAD_ROWS + c * PART, PART)] = run
            for step in (1, 0):
                move = step + 1 if side == 0 else rows - step - 1
                send(
                    totals.at[side, piece(c)], carried.at[side, step, piece(c)],
                    col_s.at[side], col_r.at[side, step, c],
                    seq_of(lax.rem(row + move, rows), pos),
                )

    def scan_second(side):
        order, seg_of = order_of(side)
        before = row if side == 0 else rows - 1 - row
        near_on = jnp.where(before >= 1, 1.0, 0.0)
        for c in range(CHUNKS):
            for step in range(2):
                arrived(carried.at[side, step, piece(c)], col_r.at[side, step, c])
            if c == 0:
                near_seg = carried[side, 0, 0:1]
                far_seg = carried[side, 1, 0:1]
                near_seg = jnp.where(before >= 1, near_seg, -1.0)
                far_on = jnp.where(before >= 2, jnp.where(far_seg == near_seg, lam_row, 0.0), 0.0)
                prev = [near_seg] + seg_of[:-1]
                factor = [jnp.where(a == b, lam, 0.0) for a, b in zip(seg_of, prev)]
            rows_c = pl.ds(HEAD_ROWS + c * PART, PART)
            part = pl.ds(c * PART, PART)
            run = carried[side, 0, rows_c] * near_on + far_on * carried[side, 1, rows_c]
            for n in range(ROW):
                prefixes[side, order[n], part] = run
                if n < ROW - 1:
                    run = gathered[side, order[n], part] + factor[n] * run
            for p in row_mates:
                send(
                    prefixes.at[side, p, part], state_in.at[side, pos, part],
                    ret_s.at[side], ret_r.at[side], seq_of(row, p),
                )
        state_in[side, pos] = prefixes[side, pos]
        return near_seg

    def scan_last(side):
        arrived(state_in.at[side, row_others], ret_r.at[side])

    loads[2].wait()
    causal = t_col >= s_row
    same = seg_col == seg_tile
    keep = jnp.logical_and(causal, same)
    for h in range(heads):
        cut = slice(h * DIM, (h + 1) * DIM)
        weights = jnp.where(keep, jnp.exp(jnp.minimum(s_row - t_col, 0.0) * inverse[h]), 0.0)
        w_ref[h] = weights
        scores = split(mm(q_ref[:, cut], k_ref[:, cut], 1, 1) * weights)
        qk_ref[h, 0] = scores[0]
        qk_ref[h, 1] = scores[1]
        att_ref[h] = mm_split_left(scores, v_ref[:, cut], 1, 0)

    arrived(meta.at[row_others], meta_r.at[0])
    scan_first(0)
    prev_row_seg = scan_second(0)
    prev_seg = jnp.where(pos == 0, prev_row_seg, meta[lax.rem(pos + ROW - 1, ROW), 0:1, :])
    loads[3].wait()
    loads[6].wait()
    scan_last(0)

    into_on = seg_col == prev_seg
    squares = jnp.zeros((BLOCK, DIM), F32)
    crosses = jnp.zeros((BLOCK, DIM), F32)
    for h in range(heads):
        cut = slice(h * DIM, (h + 1) * DIM)
        into = jnp.where(into_on, jnp.exp(-(t_col + 1.0) * inverse[h]), 0.0)
        state = split(state_in[0, 2 * h:2 * h + 2].reshape(DIM, DIM))
        att = att_ref[h] + into * mm_split_right(q_ref[:, cut], state, 1, 0)
        att_ref[h] = att
        squares = squares + att * att
        crosses = crosses + dy_ref[:, cut].astype(F32) * gain_ref[:, cut] * att
    square_row = jnp.sum(squares.T, axis=0, keepdims=True)
    cross_row = jnp.sum(crosses.T, axis=0, keepdims=True)
    z_own[0:1] = square_row
    z_own[1:2] = cross_row
    for other in z_mates:
        send(z_own, z_all.at[z], z_s.at[0], z_r.at[0], {"seq": me, "head": other})
    z_all[z] = z_own[...]
    if zs > 1:
        arrived(z_all.at[pl.ds(0, zs - 1)], z_r.at[0])
    both = z_all[0]
    for i in range(1, zs):
        both = both + z_all[i]
    inv_row = lax.rsqrt(both[0:1] / features + 1e-06)
    off_row = inv_row * inv_row * inv_row * both[1:2] / features
    inv = jnp.broadcast_to(inv_row, (BLOCK, DIM)).T
    off = jnp.broadcast_to(off_row, (BLOCK, DIM)).T

    for h in range(heads):
        cut = slice(h * DIM, (h + 1) * DIM)
        dy = dy_ref[:, cut].astype(F32)
        att = att_ref[h]
        scaled = dy * inv
        back = gain_ref[:, cut] * scaled - att * off
        back_ref[h] = back
        gr_own[h:h + 1] = jnp.sum(scaled * att, axis=0, keepdims=True)
        start = jnp.where(seg_col == first_own, jnp.exp(-t_col * inverse[h]), 0.0)
        local = mm_split_right(q_ref[:, cut], split(back * start), 0, 0)
        states[1, 2 * h] = local[:HALF]
        states[1, 2 * h + 1] = local[HALF:]
    scatter(1)
    for p in row_mates:
        send(gr_own, gr_all.at[pos], gr_s.at[0], gr_r.at[0], seq_of(row, p))
    gr_all[pos] = gr_own[...]

    def inner(h):
        cut = slice(h * DIM, (h + 1) * DIM)
        back = split(back_ref[h])
        weights = w_ref[h]
        grads = split(mm_split_left(back, v_ref[:, cut], 1, 1) * weights)
        into = jnp.where(into_on, jnp.exp(-(t_col + 1.0) * inverse[h]), 0.0)
        state = split(state_in[0, 2 * h:2 * h + 2].reshape(DIM, DIM))
        dq = mm_split_left(grads, k_ref[:, cut], 1, 0) + into * mm_split_both(back, state, 1, 1)
        dq_ref[:, cut] = dq.astype(BF16)
        dk_acc[h] = mm_split_left(grads, q_ref[:, cut], 0, 0)
        dv_acc[h] = mm_split_both((qk_ref[h, 0], qk_ref[h, 1]), back, 0, 0)

    inner(0)
    inner(1)
    scan_first(1)
    arrived(gr_all.at[row_others], gr_r.at[0])
    total = gr_all[0]
    for a in range(1, ROW):
        total = total + gr_all[a]
    gc_own[...] = total
    gc_all[row] = total
    for r in col_mates:
        send(gc_own, gc_all.at[row], gc_s.at[0], gc_r.at[0], seq_of(r, pos))
    inner(2)
    next_row_seg = scan_second(1)
    next_seg = jnp.where(pos == ROW - 1, next_row_seg, meta[lax.rem(pos + 1, ROW), 1:2, :])
    inner(3)
    arrived(gc_all.at[pl.ds(0, rows - 1)], gc_r.at[0])
    total = gc_all[0]
    for a in range(1, rows):
        total = total + gc_all[a]
    for h in range(heads):
        gg_ref[:, h * DIM:(h + 1) * DIM] = total[h:h + 1]
    scan_last(1)

    next_on = seg_col == next_seg
    for h in range(heads):
        cut = slice(h * DIM, (h + 1) * DIM)
        weight = jnp.where(next_on, jnp.exp((t_col - float(BLOCK)) * inverse[h]), 0.0)
        grad = split(state_in[1, 2 * h:2 * h + 2].reshape(DIM, DIM))
        dk = dk_acc[h] + weight * mm_split_right(v_ref[:, cut], grad, 1, 1)
        dv = dv_acc[h] + weight * mm_split_right(k_ref[:, cut], grad, 1, 0)
        dk_ref[:, cut] = dk.astype(BF16)
        dv_ref[:, cut] = dv.astype(BF16)
    sent(meta.at[row_others], meta_s.at[0])
    for side in range(2):
        sent(states.at[side, row_others], a2a_s.at[side])
        sent(carried.at[side], col_s.at[side])
        sent(prefixes.at[side, row_others], ret_s.at[side])
    if zs > 1:
        sent(z_all.at[pl.ds(0, zs - 1)], z_s.at[0])
    sent(gr_all.at[row_others], gr_s.at[0])
    sent(gc_all.at[pl.ds(0, rows - 1)], gc_s.at[0])


def store(*refs):
    count = (len(refs) - 1) // 2
    copies = [
        pltpu.make_async_copy(refs[i], refs[count + i], refs[-1].at[i]) for i in range(count)
    ]
    for copy in copies:
        copy.start()
    for copy in copies:
        copy.wait()


def local(queries, key_rows, value_rows, segment_ids, decay_span, norm_gain, out_grad):
    rows = lax.axis_size("seq") // ROW
    zs = lax.axis_size("head")
    heads = decay_span.shape[0]
    width = heads * DIM
    far = pl.BlockSpec(memory_space=pl.ANY)
    near = pl.BlockSpec(memory_space=pltpu.VMEM)
    wide = pltpu.VMEM((BLOCK, width), BF16)
    square = pltpu.VMEM((heads, DIM, DIM), F32)
    pieces = pltpu.VMEM((2, ROW, HALF, DIM), F32)
    dma = pltpu.SemaphoreType.DMA
    kept = pltpu.VMEM((1, width), F32)
    results = pl.pallas_call(
        functools.partial(kernel, rows, zs, heads),
        out_shape=(wide, wide, wide, kept),
        in_specs=[far] * 7,
        out_specs=(near,) * 4,
        scratch_shapes=[
            wide, wide, wide, wide,
            pltpu.VMEM((1, BLOCK), jnp.int32), pltpu.SMEM((heads,), F32), kept,
            pltpu.VMEM((8, DIM), F32),
            pltpu.VMEM((ROW, 8, DIM), F32),
            pieces,
            pieces,
            pltpu.VMEM((2, HEAD_ROWS + HALF, DIM), F32),
            pltpu.VMEM((2, 2, HEAD_ROWS + HALF, DIM), F32),
            pieces,
            pieces,
            pltpu.VMEM((2, DIM), F32),
            pltpu.VMEM((zs, 2, DIM), F32),
            pltpu.VMEM((heads, DIM), F32),
            pltpu.VMEM((ROW, heads, DIM), F32),
            pltpu.VMEM((heads, DIM), F32),
            pltpu.VMEM((rows, heads, DIM), F32),
            square, square, square, square, square,
            pltpu.VMEM((heads, 2, DIM, DIM), BF16),
            dma((7,)),
            dma((1,)), dma((1,)),
            dma((2,)), dma((2, CHUNKS)),
            dma((2,)), dma((2, 2, CHUNKS)),
            dma((2,)), dma((2,)),
            dma((1,)), dma((1,)),
            dma((1,)), dma((1,)),
            dma((1,)), dma((1,)),
        ],
        compiler_params=pltpu.CompilerParams(collective_id=0, has_side_effects=True),
    )(
        queries, key_rows, value_rows, out_grad,
        segment_ids.reshape(1, BLOCK), decay_span, norm_gain.reshape(1, width),
    )
    out = jax.ShapeDtypeStruct((BLOCK, width), BF16)
    dq, dk, dv, gg = pl.pallas_call(
        store,
        out_shape=(out, out, out, jax.ShapeDtypeStruct((1, width), F32)),
        in_specs=[near] * 4,
        out_specs=(far,) * 4,
        scratch_shapes=[dma((4,))],
    )(*[pltpu.with_memory_space_constraint(r, pltpu.VMEM) for r in results])
    return dq, dk, dv, gg.reshape(width)


def solution(mesh):
    in_specs = (
        P("seq", "head"),
        P("seq", "head"),
        P("seq", "head"),
        P("seq"),
        P("head"),
        P("head"),
        P("seq", "head"),
    )
    out_specs = (P("seq", "head"), P("seq", "head"), P("seq", "head"), P("head"))
    return jax.shard_map(local, mesh=mesh, in_specs=in_specs, out_specs=out_specs, check_vma=False)
```

```python
import functools

import jax
import jax.numpy as jnp
from jax import lax
from jax.experimental import pallas as pl
from jax.experimental.pallas import tpu as pltpu
from jax.sharding import PartitionSpec as P

DIM = 128
ROW = 8
BLOCK = 128
HALF = 64
CHUNKS = 4
PART = HALF // CHUNKS
HEAD_ROWS = 8
MESH = pl.DeviceIdType.MESH
F32 = jnp.float32
BF16 = jnp.bfloat16
ORDER = (4, 3, 5, 2, 6, 1, 7)


def split(x):
    high = x.astype(BF16)
    return high, (x - high.astype(F32)).astype(BF16)


def mm(a, b, ca, cb):
    return lax.dot_general(a, b, (((ca,), (cb,)), ((), ())), preferred_element_type=F32)


def mm_split_left(a, b, ca, cb):
    return mm(a[0], b, ca, cb) + mm(a[1], b, ca, cb)


def mm_split_right(a, b, ca, cb):
    return mm(a, b[0], ca, cb) + mm(a, b[1], ca, cb)


def mm_split_both(a, b, ca, cb):
    return mm(a[0], b[0], ca, cb) + (mm(a[0], b[1], ca, cb) + mm(a[1], b[0], ca, cb))


def kernel(
    rows, zs, heads,
    q_hbm, k_hbm, v_hbm, dy_hbm, seg_hbm, span_hbm, gain_hbm,
    dq_ref, dk_ref, dv_ref, gg_ref,
    q_ref, k_ref, v_ref, dy_ref, seg_ref, span_ref, gain_ref,
    meta_own, meta, states, gathered, totals, carried, prefixes, state_in,
    z_own, z_all, gr_own, gr_all, gc_own, gc_all,
    att_ref, back_ref, w_ref, dk_acc, dv_acc, qk_ref,
    in_sem, meta_s, meta_r, a2a_s, a2a_r, col_s, col_r, ret_s, ret_r,
    z_s, z_r, gr_s, gr_r, gc_s, gc_r, tokens,
):
    me = lax.axis_index("seq")
    z = lax.axis_index("head")
    row = me // ROW
    pos = lax.rem(me, ROW)
    features = float(zs * heads * DIM)

    loads = [
        pltpu.make_async_copy(src, dst, in_sem.at[i])
        for i, (src, dst) in enumerate(
            (
                (k_hbm, k_ref), (v_hbm, v_ref), (q_hbm, q_ref), (dy_hbm, dy_ref),
                (seg_hbm, seg_ref), (span_hbm, span_ref), (gain_hbm, gain_ref),
            )
        )
    ]
    for i in (4, 5, 0, 1, 2, 3, 6):
        loads[i].start()

    def seq_of(r, p):
        return {"seq": r * ROW + p, "head": z}

    row_mates = [lax.rem(pos + s, ROW) for s in ORDER]
    col_mates = [lax.rem(row + s, rows) for s in range(1, rows)]
    z_mates = [lax.rem(z + s, zs) for s in sorted(range(1, zs), key=lambda s: -min(s, zs - s))]
    z_sides = sorted({1 % zs, (zs - 1) % zs} - {0})
    up, down = row < rows - 1, row > 0
    y_sides = ((up, row + 1), (down, row - 1))
    barrier = pltpu.get_barrier_semaphore()
    for p in row_mates:
        pl.semaphore_signal(barrier, inc=1, device_id=seq_of(row, p), device_id_type=MESH)
    for s in z_sides:
        other = {"seq": me, "head": lax.rem(z + s, zs)}
        pl.semaphore_signal(barrier, inc=1, device_id=other, device_id_type=MESH)
    for near, other in y_sides:
        @pl.when(near)
        def _():
            pl.semaphore_signal(barrier, inc=1, device_id=seq_of(other, pos), device_id_type=MESH)

    y_waves, z_waves = rows - 2, zs // 2 - 1

    def token(wave):
        if wave < z_waves:
            for i, s in enumerate(z_sides):
                pl.semaphore_signal(
                    tokens.at[1, i, wave], inc=1, device_id_type=MESH,
                    device_id={"seq": me, "head": lax.rem(z + s, zs)},
                )
        if wave < y_waves:
            for i, (near, other) in enumerate(y_sides):
                @pl.when(near)
                def _():
                    pl.semaphore_signal(
                        tokens.at[0, i, wave], inc=1, device_id_type=MESH,
                        device_id=seq_of(other, pos),
                    )

    def take(wave):
        if wave < z_waves:
            for i in range(len(z_sides)):
                pl.semaphore_wait(tokens.at[1, i, wave], 1)
        if wave < y_waves:
            for i, near in enumerate((down, up)):
                @pl.when(near)
                def _():
                    pl.semaphore_wait(tokens.at[0, i, wave], 1)

    def step_tokens(wave):
        take(wave)
        token(wave + 1)

    def remote(src, dst, ss, rs, target):
        return pltpu.make_async_remote_copy(
            src_ref=src, dst_ref=dst, send_sem=ss, recv_sem=rs,
            device_id=target, device_id_type=MESH,
        )

    def send(*args):
        remote(*args).start()

    def arrived(buffer, rs):
        remote(buffer, buffer, rs, rs, seq_of(row, row_mates[0])).wait_recv()

    def sent(buffer, ss):
        remote(buffer, buffer, ss, ss, seq_of(row, row_mates[0])).wait_send()

    row_others = pl.ds(0, ROW - 1)
    loads[4].wait()
    loads[5].wait()

    t_col = lax.broadcasted_iota(jnp.int32, (BLOCK, DIM), 0).astype(F32)
    s_row = lax.broadcasted_iota(jnp.int32, (BLOCK, DIM), 1).astype(F32)
    seg_row = seg_ref[...].astype(F32)
    seg_tile = jnp.broadcast_to(seg_row, (BLOCK, DIM))
    seg_col = seg_tile.T
    first_own = jnp.broadcast_to(seg_row[:, 0:1], (1, DIM))
    last_own = jnp.broadcast_to(seg_row[:, BLOCK - 1:BLOCK], (1, DIM))
    tile_row = lax.broadcasted_iota(jnp.int32, (8, DIM), 0)
    meta_own[...] = jnp.where(tile_row == 0, last_own, first_own)
    meta[pos] = meta_own[...]

    inverse = [1.0 / jnp.full((1, DIM), span_ref[h], F32) for h in range(heads)]
    own_inverse = 1.0 / jnp.full((1, DIM), span_ref[pos // 2], F32)
    lam = jnp.exp(-float(BLOCK) * own_inverse)
    lam_row = jnp.exp(-float(BLOCK * ROW) * own_inverse)

    loads[0].wait()
    loads[1].wait()
    for h in range(heads):
        cut = slice(h * DIM, (h + 1) * DIM)
        tail = jnp.where(seg_col == last_own, jnp.exp((t_col - (BLOCK - 1.0)) * inverse[h]), 0.0)
        local = mm_split_right(
            k_ref[:, cut], split(v_ref[:, cut].astype(F32) * tail), 0, 0
        )
        states[0, 2 * h] = local[:HALF]
        states[0, 2 * h + 1] = local[HALF:]

    pl.semaphore_wait(
        barrier, len(row_mates) + len(z_sides) + up.astype(jnp.int32) + down.astype(jnp.int32)
    )

    def scatter(side):
        for c in range(CHUNKS):
            part = pl.ds(c * PART, PART)
            for p in row_mates:
                send(
                    states.at[side, p, part], gathered.at[side, pos, part],
                    a2a_s.at[side], a2a_r.at[side, c], seq_of(row, p),
                )
        gathered[side, pos] = states[side, pos]

    def piece(c):
        return pl.ds(HEAD_ROWS + c * PART, PART) if c else pl.ds(0, HEAD_ROWS + PART)

    def order_of(side):
        order = list(range(ROW)) if side == 0 else list(range(ROW - 1, -1, -1))
        return order, [meta[a, side:side + 1, :] for a in order]

    for p in row_mates:
        send(meta_own, meta.at[pos], meta_s.at[0], meta_r.at[0], seq_of(row, p))
    scatter(0)

    def before_of(side):
        return row if side == 0 else rows - 1 - row

    def after_of(side):
        return rows - 1 - row if side == 0 else row

    token(0)
    for side in range(2):
        for step in range(2):
            @pl.when(before_of(side) <= step)
            def _():
                carried[side, step, :HEAD_ROWS] = jnp.full((HEAD_ROWS, DIM), -1.0, F32)
                carried[side, step, HEAD_ROWS:] = jnp.zeros((HALF, DIM), F32)

    def scan_first(side):
        order, seg_of = order_of(side)
        factor = [jnp.where(seg_of[n] == seg_of[n - 1], lam, 0.0) for n in range(1, ROW)]
        for c in range(CHUNKS):
            part = pl.ds(c * PART, PART)
            arrived(gathered.at[side, row_others, part], a2a_r.at[side, c])
            run = gathered[side, order[0], part]
            for n in range(1, ROW):
                run = gathered[side, order[n], part] + factor[n - 1] * run
            if c == 0:
                totals[side, :HEAD_ROWS] = jnp.broadcast_to(seg_of[-1], (HEAD_ROWS, DIM))
            totals[side, pl.ds(HEAD_ROWS + c * PART, PART)] = run
            for step in (1, 0):
                @pl.when(after_of(side) > step)
                def _():
                    send(
                        totals.at[side, piece(c)], carried.at[side, step, piece(c)],
                        col_s.at[side, step], col_r.at[side, step, c],
                        seq_of(row + (step + 1 if side == 0 else -step - 1), pos),
                    )

    def scan_second(side):
        order, seg_of = order_of(side)
        for c in range(CHUNKS):
            for step in range(2):
                @pl.when(before_of(side) > step)
                def _():
                    arrived(carried.at[side, step, piece(c)], col_r.at[side, step, c])
            if c == 0:
                near_seg = carried[side, 0, 0:1]
                far_seg = carried[side, 1, 0:1]
                far_on = jnp.where(far_seg == near_seg, lam_row, 0.0)
                prev = [near_seg] + seg_of[:-1]
                factor = [jnp.where(a == b, lam, 0.0) for a, b in zip(seg_of, prev)]
            rows_c = pl.ds(HEAD_ROWS + c * PART, PART)
            part = pl.ds(c * PART, PART)
            run = carried[side, 0, rows_c] + far_on * carried[side, 1, rows_c]
            for n in range(ROW):
                prefixes[side, order[n], part] = run
                if n < ROW - 1:
                    run = gathered[side, order[n], part] + factor[n] * run
            for p in row_mates:
                send(
                    prefixes.at[side, p, part], state_in.at[side, pos, part],
                    ret_s.at[side], ret_r.at[side], seq_of(row, p),
                )
        state_in[side, pos] = prefixes[side, pos]
        return near_seg

    def scan_last(side):
        arrived(state_in.at[side, row_others], ret_r.at[side])

    loads[2].wait()
    causal = t_col >= s_row
    same = seg_col == seg_tile
    keep = jnp.logical_and(causal, same)
    for h in range(heads):
        cut = slice(h * DIM, (h + 1) * DIM)
        weights = jnp.where(keep, jnp.exp(jnp.minimum(s_row - t_col, 0.0) * inverse[h]), 0.0)
        w_ref[h] = weights
        scores = split(mm(q_ref[:, cut], k_ref[:, cut], 1, 1) * weights)
        qk_ref[h, 0] = scores[0]
        qk_ref[h, 1] = scores[1]
        att_ref[h] = mm_split_left(scores, v_ref[:, cut], 1, 0)

    step_tokens(0)
    arrived(meta.at[row_others], meta_r.at[0])
    scan_first(0)
    step_tokens(1)
    prev_row_seg = scan_second(0)
    step_tokens(2)
    prev_seg = jnp.where(pos == 0, prev_row_seg, meta[lax.rem(pos + ROW - 1, ROW), 0:1, :])
    loads[3].wait()
    loads[6].wait()
    scan_last(0)
    step_tokens(3)

    into_on = seg_col == prev_seg
    squares = jnp.zeros((BLOCK, DIM), F32)
    crosses = jnp.zeros((BLOCK, DIM), F32)
    for h in range(heads):
        cut = slice(h * DIM, (h + 1) * DIM)
        into = jnp.where(into_on, jnp.exp(-(t_col + 1.0) * inverse[h]), 0.0)
        state = split(state_in[0, 2 * h:2 * h + 2].reshape(DIM, DIM))
        att = att_ref[h] + into * mm_split_right(q_ref[:, cut], state, 1, 0)
        att_ref[h] = att
        squares = squares + att * att
        crosses = crosses + dy_ref[:, cut].astype(F32) * gain_ref[:, cut] * att
    square_row = jnp.sum(squares.T, axis=0, keepdims=True)
    cross_row = jnp.sum(crosses.T, axis=0, keepdims=True)
    z_own[0:1] = square_row
    z_own[1:2] = cross_row
    for other in z_mates:
        send(z_own, z_all.at[z], z_s.at[0], z_r.at[0], {"seq": me, "head": other})
    z_all[z] = z_own[...]
    if zs > 1:
        arrived(z_all.at[pl.ds(0, zs - 1)], z_r.at[0])
    step_tokens(4)
    both = z_all[0]
    for i in range(1, zs):
        both = both + z_all[i]
    inv_row = lax.rsqrt(both[0:1] / features + 1e-06)
    off_row = inv_row * inv_row * inv_row * both[1:2] / features
    inv = jnp.broadcast_to(inv_row, (BLOCK, DIM)).T
    off = jnp.broadcast_to(off_row, (BLOCK, DIM)).T

    for h in range(heads):
        cut = slice(h * DIM, (h + 1) * DIM)
        dy = dy_ref[:, cut].astype(F32)
        att = att_ref[h]
        scaled = dy * inv
        back = gain_ref[:, cut] * scaled - att * off
        back_ref[h] = back
        gr_own[h:h + 1] = jnp.sum(scaled * att, axis=0, keepdims=True)
        start = jnp.where(seg_col == first_own, jnp.exp(-t_col * inverse[h]), 0.0)
        local = mm_split_right(q_ref[:, cut], split(back * start), 0, 0)
        states[1, 2 * h] = local[:HALF]
        states[1, 2 * h + 1] = local[HALF:]
    scatter(1)
    for p in row_mates:
        send(gr_own, gr_all.at[pos], gr_s.at[0], gr_r.at[0], seq_of(row, p))
    gr_all[pos] = gr_own[...]

    def inner(h):
        cut = slice(h * DIM, (h + 1) * DIM)
        back = split(back_ref[h])
        weights = w_ref[h]
        grads = split(mm_split_left(back, v_ref[:, cut], 1, 1) * weights)
        into = jnp.where(into_on, jnp.exp(-(t_col + 1.0) * inverse[h]), 0.0)
        state = split(state_in[0, 2 * h:2 * h + 2].reshape(DIM, DIM))
        dq = mm_split_left(grads, k_ref[:, cut], 1, 0) + into * mm_split_both(back, state, 1, 1)
        dq_ref[:, cut] = dq.astype(BF16)
        dk_acc[h] = mm_split_left(grads, q_ref[:, cut], 0, 0)
        dv_acc[h] = mm_split_both((qk_ref[h, 0], qk_ref[h, 1]), back, 0, 0)

    inner(0)
    inner(1)
    scan_first(1)
    step_tokens(5)
    arrived(gr_all.at[row_others], gr_r.at[0])
    total = gr_all[0]
    for a in range(1, ROW):
        total = total + gr_all[a]
    gc_own[...] = total
    gc_all[row] = total
    for r in col_mates:
        send(gc_own, gc_all.at[row], gc_s.at[0], gc_r.at[0], seq_of(r, pos))
    inner(2)
    next_row_seg = scan_second(1)
    next_seg = jnp.where(pos == ROW - 1, next_row_seg, meta[lax.rem(pos + 1, ROW), 1:2, :])
    inner(3)
    arrived(gc_all.at[pl.ds(0, rows - 1)], gc_r.at[0])
    total = gc_all[0]
    for a in range(1, rows):
        total = total + gc_all[a]
    for h in range(heads):
        gg_ref[:, h * DIM:(h + 1) * DIM] = total[h:h + 1]
    scan_last(1)

    next_on = seg_col == next_seg
    for h in range(heads):
        cut = slice(h * DIM, (h + 1) * DIM)
        weight = jnp.where(next_on, jnp.exp((t_col - float(BLOCK)) * inverse[h]), 0.0)
        grad = split(state_in[1, 2 * h:2 * h + 2].reshape(DIM, DIM))
        dk = dk_acc[h] + weight * mm_split_right(v_ref[:, cut], grad, 1, 1)
        dv = dv_acc[h] + weight * mm_split_right(k_ref[:, cut], grad, 1, 0)
        dk_ref[:, cut] = dk.astype(BF16)
        dv_ref[:, cut] = dv.astype(BF16)
    sent(meta.at[row_others], meta_s.at[0])
    for side in range(2):
        sent(states.at[side, row_others], a2a_s.at[side])
        for step in range(2):
            @pl.when(after_of(side) > step)
            def _():
                sent(carried.at[side, step], col_s.at[side, step])
        sent(prefixes.at[side, row_others], ret_s.at[side])
    if zs > 1:
        sent(z_all.at[pl.ds(0, zs - 1)], z_s.at[0])
    sent(gr_all.at[row_others], gr_s.at[0])
    sent(gc_all.at[pl.ds(0, rows - 1)], gc_s.at[0])


def store(*refs):
    count = (len(refs) - 1) // 2
    copies = [
        pltpu.make_async_copy(refs[i], refs[count + i], refs[-1].at[i]) for i in range(count)
    ]
    for copy in copies:
        copy.start()
    for copy in copies:
        copy.wait()


def local(queries, key_rows, value_rows, segment_ids, decay_span, norm_gain, out_grad):
    rows = lax.axis_size("seq") // ROW
    zs = lax.axis_size("head")
    heads = decay_span.shape[0]
    width = heads * DIM
    far = pl.BlockSpec(memory_space=pl.ANY)
    near = pl.BlockSpec(memory_space=pltpu.VMEM)
    wide = pltpu.VMEM((BLOCK, width), BF16)
    square = pltpu.VMEM((heads, DIM, DIM), F32)
    pieces = pltpu.VMEM((2, ROW, HALF, DIM), F32)
    dma = pltpu.SemaphoreType.DMA
    kept = pltpu.VMEM((1, width), F32)
    results = pl.pallas_call(
        functools.partial(kernel, rows, zs, heads),
        out_shape=(wide, wide, wide, kept),
        in_specs=[far] * 7,
        out_specs=(near,) * 4,
        scratch_shapes=[
            wide, wide, wide, wide,
            pltpu.VMEM((1, BLOCK), jnp.int32), pltpu.SMEM((heads,), F32), kept,
            pltpu.VMEM((8, DIM), F32),
            pltpu.VMEM((ROW, 8, DIM), F32),
            pieces,
            pieces,
            pltpu.VMEM((2, HEAD_ROWS + HALF, DIM), F32),
            pltpu.VMEM((2, 2, HEAD_ROWS + HALF, DIM), F32),
            pieces,
            pieces,
            pltpu.VMEM((2, DIM), F32),
            pltpu.VMEM((zs, 2, DIM), F32),
            pltpu.VMEM((heads, DIM), F32),
            pltpu.VMEM((ROW, heads, DIM), F32),
            pltpu.VMEM((heads, DIM), F32),
            pltpu.VMEM((rows, heads, DIM), F32),
            square, square, square, square, square,
            pltpu.VMEM((heads, 2, DIM, DIM), BF16),
            dma((7,)),
            dma((1,)), dma((1,)),
            dma((2,)), dma((2, CHUNKS)),
            dma((2, 2)), dma((2, 2, CHUNKS)),
            dma((2,)), dma((2,)),
            dma((1,)), dma((1,)),
            dma((1,)), dma((1,)),
            dma((1,)), dma((1,)),
            pltpu.SemaphoreType.REGULAR((2, 2, 6)),
        ],
        compiler_params=pltpu.CompilerParams(collective_id=0, has_side_effects=True),
    )(
        queries, key_rows, value_rows, out_grad,
        segment_ids.reshape(1, BLOCK), decay_span, norm_gain.reshape(1, width),
    )
    out = jax.ShapeDtypeStruct((BLOCK, width), BF16)
    dq, dk, dv, gg = pl.pallas_call(
        store,
        out_shape=(out, out, out, jax.ShapeDtypeStruct((1, width), F32)),
        in_specs=[near] * 4,
        out_specs=(far,) * 4,
        scratch_shapes=[dma((4,))],
    )(*[pltpu.with_memory_space_constraint(r, pltpu.VMEM) for r in results])
    return dq, dk, dv, gg.reshape(width)


def solution(mesh):
    in_specs = (
        P("seq", "head"),
        P("seq", "head"),
        P("seq", "head"),
        P("seq"),
        P("head"),
        P("head"),
        P("seq", "head"),
    )
    out_specs = (P("seq", "head"), P("seq", "head"), P("seq", "head"), P("head"))
    return jax.shard_map(local, mesh=mesh, in_specs=in_specs, out_specs=out_specs, check_vma=False)
```

```python
import functools

import jax
import jax.numpy as jnp
from jax import lax
from jax.experimental import pallas as pl
from jax.experimental.pallas import tpu as pltpu
from jax.sharding import PartitionSpec as P

DIM = 128
ROW = 8
BLOCK = 128
CHIPS = ROW // 2
CHUNKS = 4
PART = DIM // CHUNKS
HEAD_ROWS = 8
MESH = pl.DeviceIdType.MESH
F32 = jnp.float32
BF16 = jnp.bfloat16
ORDER = (4, 3, 5, 2, 6, 1, 7)


def split(x):
    high = x.astype(BF16)
    return high, (x - high.astype(F32)).astype(BF16)


def mm(a, b, ca, cb):
    return lax.dot_general(a, b, (((ca,), (cb,)), ((), ())), preferred_element_type=F32)


def mm_split_left(a, b, ca, cb):
    return mm(a[0], b, ca, cb) + mm(a[1], b, ca, cb)


def mm_split_right(a, b, ca, cb):
    return mm(a, b[0], ca, cb) + mm(a, b[1], ca, cb)


def mm_split_both(a, b, ca, cb):
    return mm(a[0], b[0], ca, cb) + (mm(a[0], b[1], ca, cb) + mm(a[1], b[0], ca, cb))


def kernel(
    rows, zs, heads,
    q_hbm, k_hbm, v_hbm, dy_hbm, seg_hbm, span_hbm, gain_hbm,
    dq_ref, dk_ref, dv_ref, gg_ref,
    q_ref, k_ref, v_ref, dy_ref, seg_ref, span_ref, gain_ref,
    meta_own, meta, states, gathered, totals, carried, prefixes, state_in,
    z_own, z_all, gr_own, gr_all, gc_own, gc_all,
    att_ref, back_ref, w_ref, dk_acc, dv_acc, qk_ref,
    in_sem, meta_s, meta_r, a2a_s, a2a_r, col_s, col_r, ret_s, ret_r,
    z_s, z_r, gr_s, gr_r, gc_s, gc_r, tokens, edge, edge_s, edge_r,
):
    me = lax.axis_index("seq")
    z = lax.axis_index("head")
    row = me // ROW
    pos = lax.rem(me, ROW)
    chip, core = pos // 2, lax.rem(pos, 2)
    features = float(zs * heads * DIM)

    loads = [
        pltpu.make_async_copy(src, dst, in_sem.at[i])
        for i, (src, dst) in enumerate(
            (
                (k_hbm, k_ref), (v_hbm, v_ref), (q_hbm, q_ref), (dy_hbm, dy_ref),
                (seg_hbm, seg_ref), (span_hbm, span_ref), (gain_hbm, gain_ref),
            )
        )
    ]
    for i in (4, 5, 0, 1, 2, 3, 6):
        loads[i].start()

    def seq_of(r, p):
        return {"seq": r * ROW + p, "head": z}

    row_mates = [lax.rem(pos + s, ROW) for s in ORDER]
    col_mates = [lax.rem(row + s, rows) for s in range(1, rows)]
    z_mates = [lax.rem(z + s, zs) for s in sorted(range(1, zs), key=lambda s: -min(s, zs - s))]
    z_sides = sorted({1 % zs, (zs - 1) % zs} - {0})
    up, down = row < rows - 1, row > 0
    y_sides = ((up, row + 1), (down, row - 1))
    barrier = pltpu.get_barrier_semaphore()
    for p in row_mates:
        pl.semaphore_signal(barrier, inc=1, device_id=seq_of(row, p), device_id_type=MESH)
    for s in z_sides:
        other = {"seq": me, "head": lax.rem(z + s, zs)}
        pl.semaphore_signal(barrier, inc=1, device_id=other, device_id_type=MESH)
    for near, other in y_sides:
        @pl.when(near)
        def _():
            pl.semaphore_signal(barrier, inc=1, device_id=seq_of(other, pos), device_id_type=MESH)

    y_waves, z_waves = rows - 2, zs // 2 - 1

    def token(wave):
        if wave < z_waves:
            for i, s in enumerate(z_sides):
                pl.semaphore_signal(
                    tokens.at[1, i, wave], inc=1, device_id_type=MESH,
                    device_id={"seq": me, "head": lax.rem(z + s, zs)},
                )
        if wave < y_waves:
            for i, (near, other) in enumerate(y_sides):
                @pl.when(near)
                def _():
                    pl.semaphore_signal(
                        tokens.at[0, i, wave], inc=1, device_id_type=MESH,
                        device_id=seq_of(other, pos),
                    )

    def take(wave):
        if wave < z_waves:
            for i in range(len(z_sides)):
                pl.semaphore_wait(tokens.at[1, i, wave], 1)
        if wave < y_waves:
            for i, near in enumerate((down, up)):
                @pl.when(near)
                def _():
                    pl.semaphore_wait(tokens.at[0, i, wave], 1)

    def step_tokens(wave):
        take(wave)
        token(wave + 1)

    def remote(src, dst, ss, rs, target):
        return pltpu.make_async_remote_copy(
            src_ref=src, dst_ref=dst, send_sem=ss, recv_sem=rs,
            device_id=target, device_id_type=MESH,
        )

    def send(*args):
        remote(*args).start()

    def arrived(buffer, rs):
        remote(buffer, buffer, rs, rs, seq_of(row, row_mates[0])).wait_recv()

    def sent(buffer, ss):
        remote(buffer, buffer, ss, ss, seq_of(row, row_mates[0])).wait_send()

    row_others = pl.ds(0, ROW - 1)
    loads[4].wait()
    loads[5].wait()

    t_col = lax.broadcasted_iota(jnp.int32, (BLOCK, DIM), 0).astype(F32)
    s_row = lax.broadcasted_iota(jnp.int32, (BLOCK, DIM), 1).astype(F32)
    seg_row = seg_ref[...].astype(F32)
    seg_tile = jnp.broadcast_to(seg_row, (BLOCK, DIM))
    seg_col = seg_tile.T
    first_own = jnp.broadcast_to(seg_row[:, 0:1], (1, DIM))
    last_own = jnp.broadcast_to(seg_row[:, BLOCK - 1:BLOCK], (1, DIM))
    tile_row = lax.broadcasted_iota(jnp.int32, (8, DIM), 0)
    meta_own[...] = jnp.where(tile_row == 0, last_own, first_own)
    meta[pos] = meta_own[...]

    inverse = [1.0 / jnp.full((1, DIM), span_ref[h], F32) for h in range(heads)]
    own_inverse = 1.0 / jnp.full((1, DIM), span_ref[chip], F32)
    lam = jnp.exp(-float(BLOCK) * own_inverse)
    lam_row = jnp.exp(-float(BLOCK * ROW) * own_inverse)

    loads[0].wait()
    loads[1].wait()
    for h in range(heads):
        cut = slice(h * DIM, (h + 1) * DIM)
        tail = jnp.where(seg_col == last_own, jnp.exp((t_col - (BLOCK - 1.0)) * inverse[h]), 0.0)
        local = mm_split_right(
            k_ref[:, cut], split(v_ref[:, cut].astype(F32) * tail), 0, 0
        )
        states[0, h] = local

    pl.semaphore_wait(
        barrier, len(row_mates) + len(z_sides) + up.astype(jnp.int32) + down.astype(jnp.int32)
    )

    def scatter(side):
        for c in range(CHUNKS):
            part = pl.ds(c * PART, PART)
            for d in (2, 1, 3):
                h = lax.rem(chip + d, CHIPS)
                send(
                    states.at[side, h, part], gathered.at[side, pos, part],
                    a2a_s.at[side], a2a_r.at[side, c], seq_of(row, 2 * h + 1),
                )

            @pl.when(core == 0)
            def _():
                send(
                    states.at[side, chip, part], gathered.at[side, pos, part],
                    a2a_s.at[side], a2a_r.at[side, c], seq_of(row, pos + 1),
                )

        @pl.when(core == 1)
        def _():
            gathered[side, pos] = states[side, chip]

    def piece(c):
        return pl.ds(HEAD_ROWS + c * PART, PART) if c else pl.ds(0, HEAD_ROWS + PART)

    def order_of(side):
        order = list(range(ROW)) if side == 0 else list(range(ROW - 1, -1, -1))
        return order, [meta[a, side:side + 1, :] for a in order]

    for p in row_mates:
        send(meta_own, meta.at[pos], meta_s.at[0], meta_r.at[0], seq_of(row, p))
    scatter(0)

    def before_of(side):
        return row if side == 0 else rows - 1 - row

    def after_of(side):
        return rows - 1 - row if side == 0 else row

    token(0)
    for side in range(2):
        for step in range(2):
            @pl.when(before_of(side) <= step)
            def _():
                carried[side, step, :HEAD_ROWS] = jnp.full((HEAD_ROWS, DIM), -1.0, F32)
                carried[side, step, HEAD_ROWS:] = jnp.zeros((DIM, DIM), F32)

    def scan_first(side):
        order, seg_of = order_of(side)
        factor = [jnp.where(seg_of[n] == seg_of[n - 1], lam, 0.0) for n in range(1, ROW)]
        for c in range(CHUNKS):
            part = pl.ds(c * PART, PART)
            arrived(gathered.at[side, row_others, part], a2a_r.at[side, c])
            run = gathered[side, order[0], part]
            for n in range(1, ROW):
                run = gathered[side, order[n], part] + factor[n - 1] * run
            if c == 0:
                totals[side, :HEAD_ROWS] = jnp.broadcast_to(seg_of[-1], (HEAD_ROWS, DIM))
            totals[side, pl.ds(HEAD_ROWS + c * PART, PART)] = run
            for step in (1, 0):
                @pl.when(after_of(side) > step)
                def _():
                    send(
                        totals.at[side, piece(c)], carried.at[side, step, piece(c)],
                        col_s.at[side, step], col_r.at[side, step, c],
                        seq_of(row + (step + 1 if side == 0 else -step - 1), pos),
                    )

    def scan_second(side):
        order, seg_of = order_of(side)
        for c in range(CHUNKS):
            for step in range(2):
                @pl.when(before_of(side) > step)
                def _():
                    arrived(carried.at[side, step, piece(c)], col_r.at[side, step, c])
            if c == 0:
                if side == 0:
                    @pl.when(pos == 1)
                    def _():
                        send(carried.at[0, 0, pl.ds(0, HEAD_ROWS)], edge,
                             edge_s.at[0], edge_r.at[0], seq_of(row, pos - 1))
                near_seg = carried[side, 0, 0:1]
                far_seg = carried[side, 1, 0:1]
                far_on = jnp.where(far_seg == near_seg, lam_row, 0.0)
                prev = [near_seg] + seg_of[:-1]
                factor = [jnp.where(a == b, lam, 0.0) for a, b in zip(seg_of, prev)]
            rows_c = pl.ds(HEAD_ROWS + c * PART, PART)
            part = pl.ds(c * PART, PART)
            run = carried[side, 0, rows_c] + far_on * carried[side, 1, rows_c]
            for n in range(ROW):
                prefixes[side, order[n], part] = run
                if n < ROW - 1:
                    run = gathered[side, order[n], part] + factor[n] * run
            for p in row_mates:
                send(
                    prefixes.at[side, p, part], state_in.at[side, chip, part],
                    ret_s.at[side], ret_r.at[side], seq_of(row, p),
                )
        state_in[side, chip] = prefixes[side, pos]

    def scan_last(side):
        @pl.when(core == 0)
        def _():
            arrived(state_in.at[side], ret_r.at[side])

        @pl.when(core == 1)
        def _():
            arrived(state_in.at[side, pl.ds(0, CHIPS - 1)], ret_r.at[side])

    loads[2].wait()
    causal = t_col >= s_row
    same = seg_col == seg_tile
    keep = jnp.logical_and(causal, same)
    for h in range(heads):
        cut = slice(h * DIM, (h + 1) * DIM)
        weights = jnp.where(keep, jnp.exp(jnp.minimum(s_row - t_col, 0.0) * inverse[h]), 0.0)
        w_ref[h] = weights
        scores = split(mm(q_ref[:, cut], k_ref[:, cut], 1, 1) * weights)
        qk_ref[h, 0] = scores[0]
        qk_ref[h, 1] = scores[1]
        att_ref[h] = mm_split_left(scores, v_ref[:, cut], 1, 0)

    step_tokens(0)
    arrived(meta.at[row_others], meta_r.at[0])
    pl.when(core == 1)(lambda: scan_first(0))
    step_tokens(1)
    pl.when(core == 1)(lambda: scan_second(0))
    step_tokens(2)
    loads[3].wait()
    loads[6].wait()
    scan_last(0)
    step_tokens(3)

    @pl.when(pos == 0)
    def _():
        arrived(edge, edge_r.at[0])

    prev_seg = jnp.where(pos == 0, edge[0:1], meta[lax.rem(pos + ROW - 1, ROW), 0:1, :])

    into_on = seg_col == prev_seg
    squares = jnp.zeros((BLOCK, DIM), F32)
    crosses = jnp.zeros((BLOCK, DIM), F32)
    for h in range(heads):
        cut = slice(h * DIM, (h + 1) * DIM)
        into = jnp.where(into_on, jnp.exp(-(t_col + 1.0) * inverse[h]), 0.0)
        state = split(state_in[0, h])
        att = att_ref[h] + into * mm_split_right(q_ref[:, cut], state, 1, 0)
        att_ref[h] = att
        squares = squares + att * att
        crosses = crosses + dy_ref[:, cut].astype(F32) * gain_ref[:, cut] * att
    square_row = jnp.sum(squares.T, axis=0, keepdims=True)
    cross_row = jnp.sum(crosses.T, axis=0, keepdims=True)
    z_own[0:1] = square_row
    z_own[1:2] = cross_row
    for other in z_mates:
        send(z_own, z_all.at[z], z_s.at[0], z_r.at[0], {"seq": me, "head": other})
    z_all[z] = z_own[...]
    if zs > 1:
        arrived(z_all.at[pl.ds(0, zs - 1)], z_r.at[0])
    step_tokens(4)
    both = z_all[0]
    for i in range(1, zs):
        both = both + z_all[i]
    inv_row = lax.rsqrt(both[0:1] / features + 1e-06)
    off_row = inv_row * inv_row * inv_row * both[1:2] / features
    inv = jnp.broadcast_to(inv_row, (BLOCK, DIM)).T
    off = jnp.broadcast_to(off_row, (BLOCK, DIM)).T

    for h in range(heads):
        cut = slice(h * DIM, (h + 1) * DIM)
        dy = dy_ref[:, cut].astype(F32)
        att = att_ref[h]
        scaled = dy * inv
        back = gain_ref[:, cut] * scaled - att * off
        back_ref[h] = back
        gr_own[h:h + 1] = jnp.sum(scaled * att, axis=0, keepdims=True)
        start = jnp.where(seg_col == first_own, jnp.exp(-t_col * inverse[h]), 0.0)
        local = mm_split_right(q_ref[:, cut], split(back * start), 0, 0)
        states[1, h] = local
    scatter(1)
    for p in row_mates:
        send(gr_own, gr_all.at[pos], gr_s.at[0], gr_r.at[0], seq_of(row, p))
    gr_all[pos] = gr_own[...]

    def inner(h):
        cut = slice(h * DIM, (h + 1) * DIM)
        back = split(back_ref[h])
        weights = w_ref[h]
        grads = split(mm_split_left(back, v_ref[:, cut], 1, 1) * weights)
        into = jnp.where(into_on, jnp.exp(-(t_col + 1.0) * inverse[h]), 0.0)
        state = split(state_in[0, h])
        dq = mm_split_left(grads, k_ref[:, cut], 1, 0) + into * mm_split_both(back, state, 1, 1)
        dq_ref[:, cut] = dq.astype(BF16)
        dk_acc[h] = mm_split_left(grads, q_ref[:, cut], 0, 0)
        dv_acc[h] = mm_split_both((qk_ref[h, 0], qk_ref[h, 1]), back, 0, 0)

    inner(0)
    inner(1)
    pl.when(core == 1)(lambda: scan_first(1))
    step_tokens(5)
    arrived(gr_all.at[row_others], gr_r.at[0])
    total = gr_all[0]
    for a in range(1, ROW):
        total = total + gr_all[a]
    gc_own[...] = total
    gc_all[row] = total
    for r in col_mates:
        send(gc_own, gc_all.at[row], gc_s.at[0], gc_r.at[0], seq_of(r, pos))
    inner(2)
    pl.when(core == 1)(lambda: scan_second(1))
    next_seg = jnp.where(
        pos == ROW - 1, carried[1, 0, 0:1], meta[lax.rem(pos + 1, ROW), 1:2, :]
    )
    inner(3)
    arrived(gc_all.at[pl.ds(0, rows - 1)], gc_r.at[0])
    total = gc_all[0]
    for a in range(1, rows):
        total = total + gc_all[a]
    for h in range(heads):
        gg_ref[:, h * DIM:(h + 1) * DIM] = total[h:h + 1]
    scan_last(1)

    next_on = seg_col == next_seg
    for h in range(heads):
        cut = slice(h * DIM, (h + 1) * DIM)
        weight = jnp.where(next_on, jnp.exp((t_col - float(BLOCK)) * inverse[h]), 0.0)
        grad = split(state_in[1, h])
        dk = dk_acc[h] + weight * mm_split_right(v_ref[:, cut], grad, 1, 1)
        dv = dv_acc[h] + weight * mm_split_right(k_ref[:, cut], grad, 1, 0)
        dk_ref[:, cut] = dk.astype(BF16)
        dv_ref[:, cut] = dv.astype(BF16)
    sent(meta.at[row_others], meta_s.at[0])
    for side in range(2):
        @pl.when(core == 0)
        def _():
            sent(states.at[side], a2a_s.at[side])

        @pl.when(core == 1)
        def _():
            sent(states.at[side, pl.ds(0, CHIPS - 1)], a2a_s.at[side])
            sent(prefixes.at[side, row_others], ret_s.at[side])
            for step in range(2):
                @pl.when(after_of(side) > step)
                def _():
                    sent(carried.at[side, step], col_s.at[side, step])

    @pl.when(pos == 1)
    def _():
        sent(edge, edge_s.at[0])

    if zs > 1:
        sent(z_all.at[pl.ds(0, zs - 1)], z_s.at[0])
    sent(gr_all.at[row_others], gr_s.at[0])
    sent(gc_all.at[pl.ds(0, rows - 1)], gc_s.at[0])


def store(*refs):
    count = (len(refs) - 1) // 2
    copies = [
        pltpu.make_async_copy(refs[i], refs[count + i], refs[-1].at[i]) for i in range(count)
    ]
    for copy in copies:
        copy.start()
    for copy in copies:
        copy.wait()


def local(queries, key_rows, value_rows, segment_ids, decay_span, norm_gain, out_grad):
    rows = lax.axis_size("seq") // ROW
    zs = lax.axis_size("head")
    heads = decay_span.shape[0]
    width = heads * DIM
    far = pl.BlockSpec(memory_space=pl.ANY)
    near = pl.BlockSpec(memory_space=pltpu.VMEM)
    wide = pltpu.VMEM((BLOCK, width), BF16)
    square = pltpu.VMEM((heads, DIM, DIM), F32)
    pieces = pltpu.VMEM((2, ROW, DIM, DIM), F32)
    per_head = pltpu.VMEM((2, heads, DIM, DIM), F32)
    dma = pltpu.SemaphoreType.DMA
    kept = pltpu.VMEM((1, width), F32)
    results = pl.pallas_call(
        functools.partial(kernel, rows, zs, heads),
        out_shape=(wide, wide, wide, kept),
        in_specs=[far] * 7,
        out_specs=(near,) * 4,
        scratch_shapes=[
            wide, wide, wide, wide,
            pltpu.VMEM((1, BLOCK), jnp.int32), pltpu.SMEM((heads,), F32), kept,
            pltpu.VMEM((8, DIM), F32),
            pltpu.VMEM((ROW, 8, DIM), F32),
            per_head,
            pieces,
            pltpu.VMEM((2, HEAD_ROWS + DIM, DIM), F32),
            pltpu.VMEM((2, 2, HEAD_ROWS + DIM, DIM), F32),
            pieces,
            per_head,
            pltpu.VMEM((2, DIM), F32),
            pltpu.VMEM((zs, 2, DIM), F32),
            pltpu.VMEM((heads, DIM), F32),
            pltpu.VMEM((ROW, heads, DIM), F32),
            pltpu.VMEM((heads, DIM), F32),
            pltpu.VMEM((rows, heads, DIM), F32),
            square, square, square, square, square,
            pltpu.VMEM((heads, 2, DIM, DIM), BF16),
            dma((7,)),
            dma((1,)), dma((1,)),
            dma((2,)), dma((2, CHUNKS)),
            dma((2, 2)), dma((2, 2, CHUNKS)),
            dma((2,)), dma((2,)),
            dma((1,)), dma((1,)),
            dma((1,)), dma((1,)),
            dma((1,)), dma((1,)),
            pltpu.SemaphoreType.REGULAR((2, 2, 6)),
            pltpu.VMEM((HEAD_ROWS, DIM), F32), dma((1,)), dma((1,)),
        ],
        compiler_params=pltpu.CompilerParams(collective_id=0, has_side_effects=True),
    )(
        queries, key_rows, value_rows, out_grad,
        segment_ids.reshape(1, BLOCK), decay_span, norm_gain.reshape(1, width),
    )
    out = jax.ShapeDtypeStruct((BLOCK, width), BF16)
    dq, dk, dv, gg = pl.pallas_call(
        store,
        out_shape=(out, out, out, jax.ShapeDtypeStruct((1, width), F32)),
        in_specs=[near] * 4,
        out_specs=(far,) * 4,
        scratch_shapes=[dma((4,))],
    )(*[pltpu.with_memory_space_constraint(r, pltpu.VMEM) for r in results])
    return dq, dk, dv, gg.reshape(width)


def solution(mesh):
    in_specs = (
        P("seq", "head"),
        P("seq", "head"),
        P("seq", "head"),
        P("seq"),
        P("head"),
        P("head"),
        P("seq", "head"),
    )
    out_specs = (P("seq", "head"), P("seq", "head"), P("seq", "head"), P("head"))
    return jax.shard_map(local, mesh=mesh, in_specs=in_specs, out_specs=out_specs, check_vma=False)
```

```python
import functools

import jax
import jax.numpy as jnp
from jax import lax
from jax.experimental import pallas as pl
from jax.experimental.pallas import tpu as pltpu
from jax.sharding import PartitionSpec as P

DIM = 128
ROW = 8
BLOCK = 128
CHIPS = ROW // 2
CHUNKS = 8
PART = DIM // CHUNKS
HEAD_ROWS = 8
MESH = pl.DeviceIdType.MESH
F32 = jnp.float32
BF16 = jnp.bfloat16
ORDER = (4, 3, 5, 2, 6, 1, 7)


def split(x):
    high = x.astype(BF16)
    return high, (x - high.astype(F32)).astype(BF16)


def mm(a, b, ca, cb):
    return lax.dot_general(a, b, (((ca,), (cb,)), ((), ())), preferred_element_type=F32)


def mm_split_left(a, b, ca, cb):
    return mm(a[0], b, ca, cb) + mm(a[1], b, ca, cb)


def mm_split_right(a, b, ca, cb):
    return mm(a, b[0], ca, cb) + mm(a, b[1], ca, cb)


def mm_split_both(a, b, ca, cb):
    return mm(a[0], b[0], ca, cb) + (mm(a[0], b[1], ca, cb) + mm(a[1], b[0], ca, cb))


def kernel(
    rows, zs, heads,
    q_hbm, k_hbm, v_hbm, dy_hbm, seg_hbm, span_hbm, gain_hbm,
    dq_ref, dk_ref, dv_ref, gg_ref,
    q_ref, k_ref, v_ref, dy_ref, seg_ref, span_ref, gain_ref,
    meta_own, meta, states, gathered, totals, carried, prefixes, state_in,
    z_own, z_all, gr_own, gr_all, gc_own, gc_all,
    att_ref, back_ref, w_ref, dk_acc, dv_acc, qk_ref,
    in_sem, meta_s, meta_r, a2a_s, a2a_r, col_s, col_r, ret_s, ret_r,
    z_s, z_r, gr_s, gr_r, gc_s, gc_r, tokens, edge, edge_s, edge_r,
    into_ref, next_ref, start_ref, gdy_ref, start_gdy, start_att, q_turned,
):
    me = lax.axis_index("seq")
    z = lax.axis_index("head")
    row = me // ROW
    pos = lax.rem(me, ROW)
    chip, core = pos // 2, lax.rem(pos, 2)
    features = float(zs * heads * DIM)

    loads = [
        pltpu.make_async_copy(src, dst, in_sem.at[i])
        for i, (src, dst) in enumerate(
            (
                (k_hbm, k_ref), (v_hbm, v_ref), (q_hbm, q_ref), (dy_hbm, dy_ref),
                (seg_hbm, seg_ref), (span_hbm, span_ref), (gain_hbm, gain_ref),
            )
        )
    ]
    for i in (4, 5, 0, 1, 2, 3, 6):
        loads[i].start()

    def seq_of(r, p):
        return {"seq": r * ROW + p, "head": z}

    row_mates = [lax.rem(pos + s, ROW) for s in ORDER]
    col_mates = [lax.rem(row + s, rows) for s in range(1, rows)]
    z_mates = [lax.rem(z + s, zs) for s in sorted(range(1, zs), key=lambda s: -min(s, zs - s))]
    z_sides = sorted({1 % zs, (zs - 1) % zs} - {0})
    up, down = row < rows - 1, row > 0
    y_sides = ((up, row + 1), (down, row - 1))
    barrier = pltpu.get_barrier_semaphore()
    for p in row_mates:
        pl.semaphore_signal(barrier, inc=1, device_id=seq_of(row, p), device_id_type=MESH)
    for s in z_sides:
        other = {"seq": me, "head": lax.rem(z + s, zs)}
        pl.semaphore_signal(barrier, inc=1, device_id=other, device_id_type=MESH)
    for near, other in y_sides:
        @pl.when(near)
        def _():
            pl.semaphore_signal(barrier, inc=1, device_id=seq_of(other, pos), device_id_type=MESH)

    y_waves, z_waves = rows - 2, zs // 2 - 1

    def token(wave):
        if wave < z_waves:
            for i, s in enumerate(z_sides):
                pl.semaphore_signal(
                    tokens.at[1, i], inc=1, device_id_type=MESH,
                    device_id={"seq": me, "head": lax.rem(z + s, zs)},
                )
        if wave < y_waves:
            for i, (near, other) in enumerate(y_sides):
                @pl.when(near)
                def _():
                    pl.semaphore_signal(
                        tokens.at[0, i], inc=1, device_id_type=MESH,
                        device_id=seq_of(other, pos),
                    )

    def take(wave):
        if wave < z_waves:
            for i in range(len(z_sides)):
                pl.semaphore_wait(tokens.at[1, i], 1)
        if wave < y_waves:
            for i, near in enumerate((down, up)):
                @pl.when(near)
                def _():
                    pl.semaphore_wait(tokens.at[0, i], 1)

    def step_tokens(wave):
        take(wave)
        token(wave + 1)

    def remote(src, dst, ss, rs, target):
        return pltpu.make_async_remote_copy(
            src_ref=src, dst_ref=dst, send_sem=ss, recv_sem=rs,
            device_id=target, device_id_type=MESH,
        )

    def send(*args):
        remote(*args).start()

    def arrived(buffer, rs):
        remote(buffer, buffer, rs, rs, seq_of(row, row_mates[0])).wait_recv()

    def sent(buffer, ss):
        remote(buffer, buffer, ss, ss, seq_of(row, row_mates[0])).wait_send()

    row_others = pl.ds(0, ROW - 1)
    loads[4].wait()
    loads[5].wait()

    t_col = lax.broadcasted_iota(jnp.int32, (BLOCK, DIM), 0).astype(F32)
    s_row = lax.broadcasted_iota(jnp.int32, (BLOCK, DIM), 1).astype(F32)
    seg_row = seg_ref[...].astype(F32)
    seg_tile = jnp.broadcast_to(seg_row, (BLOCK, DIM))
    seg_col = seg_tile.T
    first_own = jnp.broadcast_to(seg_row[:, 0:1], (1, DIM))
    last_own = jnp.broadcast_to(seg_row[:, BLOCK - 1:BLOCK], (1, DIM))
    meta_own[0:1] = last_own
    meta_own[1:2] = first_own
    meta[pos] = meta_own[...]

    inverse = [1.0 / jnp.full((1, DIM), span_ref[h], F32) for h in range(heads)]
    own_inverse = 1.0 / jnp.full((1, DIM), span_ref[chip], F32)
    lam = jnp.exp(-float(BLOCK) * own_inverse)
    lam_row = jnp.exp(-float(BLOCK * ROW) * own_inverse)

    for h in range(heads):
        att_ref[h] = jnp.where(
            seg_col == last_own, jnp.exp((t_col - (BLOCK - 1.0)) * inverse[h]), 0.0
        )
    loads[0].wait()
    loads[1].wait()
    for h in range(heads):
        cut = slice(h * DIM, (h + 1) * DIM)
        local = mm_split_right(
            k_ref[:, cut], split(v_ref[:, cut].astype(F32) * att_ref[h]), 0, 0
        )
        states[0, h] = local

    pl.semaphore_wait(
        barrier, len(row_mates) + len(z_sides) + up.astype(jnp.int32) + down.astype(jnp.int32)
    )

    def scatter(side):
        for c in range(CHUNKS):
            part = pl.ds(c * PART, PART)
            for d in (2, 1, 3):
                h = lax.rem(chip + d, CHIPS)
                send(
                    states.at[side, h, part], gathered.at[side, pos, part],
                    a2a_s.at[0], a2a_r.at[c], seq_of(row, 2 * h + 1),
                )

            @pl.when(core == 0)
            def _():
                send(
                    states.at[side, chip, part], gathered.at[side, pos, part],
                    a2a_s.at[0], a2a_r.at[c], seq_of(row, pos + 1),
                )

        @pl.when(core == 1)
        def _():
            gathered[side, pos] = states[side, chip]

    def piece(c):
        return pl.ds(HEAD_ROWS + c * PART, PART) if c else pl.ds(0, HEAD_ROWS + PART)

    def order_of(side):
        order = list(range(ROW)) if side == 0 else list(range(ROW - 1, -1, -1))
        return order, [meta[a, side:side + 1, :] for a in order]

    for p in row_mates:
        send(meta_own, meta.at[pos], meta_s.at[0], meta_r.at[0], seq_of(row, p))
    scatter(0)

    def before_of(side):
        return row if side == 0 else rows - 1 - row

    def after_of(side):
        return rows - 1 - row if side == 0 else row

    token(0)
    for side in range(2):
        for step in range(2):
            @pl.when(before_of(side) <= step)
            def _():
                carried[2 * side + step, :HEAD_ROWS] = jnp.full((HEAD_ROWS, DIM), -1.0, F32)
                carried[2 * side + step, HEAD_ROWS:] = jnp.zeros((DIM, DIM), F32)

    def scan_first(side):
        order, seg_of = order_of(side)
        factor = [jnp.where(seg_of[n] == seg_of[n - 1], lam, 0.0) for n in range(1, ROW)]
        for c in range(CHUNKS):
            part = pl.ds(c * PART, PART)
            arrived(gathered.at[side, row_others, part], a2a_r.at[c])
            run = gathered[side, order[0], part]
            for n in range(1, ROW):
                run = gathered[side, order[n], part] + factor[n - 1] * run
            if c == 0:
                totals[side, :HEAD_ROWS] = jnp.broadcast_to(seg_of[-1], (HEAD_ROWS, DIM))
            totals[side, pl.ds(HEAD_ROWS + c * PART, PART)] = run
            for step in (1, 0):
                @pl.when(after_of(side) > step)
                def _():
                    send(
                        totals.at[side, piece(c)], carried.at[2 * side + step, piece(c)],
                        col_s.at[0], col_r.at[side, c],
                        seq_of(row + (step + 1 if side == 0 else -step - 1), pos),
                    )

    def scan_second(side):
        order, seg_of = order_of(side)
        for c in range(CHUNKS):
            @pl.when(before_of(side) == 1)
            def _():
                arrived(carried.at[2 * side, piece(c)], col_r.at[side, c])

            @pl.when(before_of(side) > 1)
            def _():
                arrived(carried.at[pl.ds(2 * side, 2), piece(c)], col_r.at[side, c])

            if c == 0:
                if side == 0:
                    @pl.when(pos == 1)
                    def _():
                        send(carried.at[0, pl.ds(0, HEAD_ROWS)], edge,
                             edge_s.at[0], edge_r.at[0], seq_of(row, pos - 1))
                near_seg = carried[2 * side, 0:1]
                far_seg = carried[2 * side + 1, 0:1]
                far_on = jnp.where(far_seg == near_seg, lam_row, 0.0)
                prev = [near_seg] + seg_of[:-1]
                factor = [jnp.where(a == b, lam, 0.0) for a, b in zip(seg_of, prev)]
            rows_c = pl.ds(HEAD_ROWS + c * PART, PART)
            part = pl.ds(c * PART, PART)
            run = carried[2 * side, rows_c] + far_on * carried[2 * side + 1, rows_c]
            for n in range(ROW):
                prefixes[side, order[n], part] = run
                if n < ROW - 1:
                    run = gathered[side, order[n], part] + factor[n] * run
            for p in row_mates:
                send(
                    prefixes.at[side, p, part], state_in.at[side, chip, part],
                    ret_s.at[0], ret_r.at[lax.rem(chip + CHIPS - p // 2, CHIPS)],
                    seq_of(row, p),
                )
        state_in[side, chip] = prefixes[side, pos]

    def next_head(side, d):
        head = lax.rem(chip + d, CHIPS)
        if d:
            arrived(state_in.at[side, head], ret_r.at[d])
        else:
            @pl.when(core == 0)
            def _():
                arrived(state_in.at[side, head], ret_r.at[d])
        return head, pl.ds(pl.multiple_of(head * DIM, DIM), DIM)

    loads[2].wait()
    causal = t_col >= s_row
    same = seg_col == seg_tile
    keep = jnp.logical_and(causal, same)
    for h in range(heads):
        cut = slice(h * DIM, (h + 1) * DIM)
        weights = jnp.where(keep, jnp.exp(jnp.minimum(s_row - t_col, 0.0) * inverse[h]), 0.0)
        w_ref[h] = weights
        scores = split(mm(q_ref[:, cut], k_ref[:, cut], 1, 1) * weights)
        qk_ref[h, 0] = scores[0]
        qk_ref[h, 1] = scores[1]
        att_ref[h] = mm_split_left(scores, v_ref[:, cut], 1, 0)
        into_ref[h] = jnp.exp(-(t_col + 1.0) * inverse[h])
        next_ref[h] = jnp.exp((t_col - float(BLOCK)) * inverse[h])
        start_ref[h] = jnp.where(seg_col == first_own, jnp.exp(-t_col * inverse[h]), 0.0)

    loads[3].wait()
    loads[6].wait()
    for h in range(heads):
        cut = slice(h * DIM, (h + 1) * DIM)
        gdy_ref[h] = gain_ref[:, cut] * dy_ref[:, cut].astype(F32)
    step_tokens(0)
    arrived(meta.at[row_others], meta_r.at[0])
    pl.when(core == 1)(lambda: scan_first(0))
    step_tokens(1)
    pl.when(core == 1)(lambda: scan_second(0))
    step_tokens(2)
    step_tokens(3)

    @pl.when(pos == 0)
    def _():
        arrived(edge, edge_r.at[0])

    prev_seg = jnp.where(pos == 0, edge[0:1], meta[lax.rem(pos + ROW - 1, ROW), 0:1, :])
    into_on = seg_col == prev_seg
    for h in range(heads):
        into_ref[h] = jnp.where(into_on, into_ref[h], 0.0)
    squares = jnp.zeros((BLOCK, DIM), F32)
    crosses = jnp.zeros((BLOCK, DIM), F32)
    for d in (0, 1, 3, 2):
        h, cut = next_head(0, d)
        state = split(state_in[0, h])
        att = att_ref[h] + into_ref[h] * mm_split_right(q_ref[:, cut], state, 1, 0)
        att_ref[h] = att
        squares = squares + att * att
        crosses = crosses + gdy_ref[h] * att
    square_row = jnp.sum(squares.T, axis=0, keepdims=True)
    cross_row = jnp.sum(crosses.T, axis=0, keepdims=True)
    z_own[0:1] = square_row
    z_own[1:2] = cross_row
    for other in z_mates:
        send(z_own, z_all.at[z], z_s.at[0], z_r.at[0], {"seq": me, "head": other})
    z_all[z] = z_own[...]
    for h in range(heads):
        start_gdy[h] = start_ref[h] * gdy_ref[h]
        start_att[h] = start_ref[h] * att_ref[h]
        q_turned[h] = q_ref[:, h * DIM:(h + 1) * DIM].T
    if zs > 1:
        arrived(z_all.at[pl.ds(0, zs - 1)], z_r.at[0])
    step_tokens(4)
    both = z_all[0]
    for i in range(1, zs):
        both = both + z_all[i]
    inv_row = lax.rsqrt(both[0:1] / features + 1e-06)
    off_row = inv_row * inv_row * inv_row * both[1:2] / features
    inv = jnp.broadcast_to(inv_row, (BLOCK, DIM)).T
    off = jnp.broadcast_to(off_row, (BLOCK, DIM)).T

    for h in range(heads):
        scaled = split(inv * start_gdy[h] - off * start_att[h])
        states[1, h] = mm_split_right(q_turned[h], scaled, 1, 0)
    scatter(1)
    for h in range(heads):
        cut = slice(h * DIM, (h + 1) * DIM)
        att = att_ref[h]
        back_ref[h] = gdy_ref[h] * inv - att * off
        gr_own[h:h + 1] = jnp.sum(dy_ref[:, cut].astype(F32) * inv * att, axis=0, keepdims=True)
    for p in row_mates:
        send(gr_own, gr_all.at[pos], gr_s.at[0], gr_r.at[0], seq_of(row, p))
    gr_all[pos] = gr_own[...]

    def inner(h):
        cut = slice(h * DIM, (h + 1) * DIM)
        back = split(back_ref[h])
        weights = w_ref[h]
        grads = split(mm_split_left(back, v_ref[:, cut], 1, 1) * weights)
        into = into_ref[h]
        state = split(state_in[0, h])
        dq = mm_split_left(grads, k_ref[:, cut], 1, 0) + into * mm_split_both(back, state, 1, 1)
        dq_ref[:, cut] = dq.astype(BF16)
        dk_acc[h] = mm_split_left(grads, q_ref[:, cut], 0, 0)
        dv_acc[h] = mm_split_both((qk_ref[h, 0], qk_ref[h, 1]), back, 0, 0)

    inner(0)
    inner(1)
    pl.when(core == 1)(lambda: scan_first(1))
    step_tokens(5)
    arrived(gr_all.at[row_others], gr_r.at[0])
    total = gr_all[0]
    for a in range(1, ROW):
        total = total + gr_all[a]
    gc_own[...] = total
    gc_all[row] = total
    for r in col_mates:
        send(gc_own, gc_all.at[row], gc_s.at[0], gc_r.at[0], seq_of(r, pos))
    inner(2)
    pl.when(core == 1)(lambda: scan_second(1))
    next_seg = jnp.where(
        pos == ROW - 1, carried[2, 0:1], meta[lax.rem(pos + 1, ROW), 1:2, :]
    )
    inner(3)
    arrived(gc_all.at[pl.ds(0, rows - 1)], gc_r.at[0])
    total = gc_all[0]
    for a in range(1, rows):
        total = total + gc_all[a]
    for h in range(heads):
        gg_ref[:, h * DIM:(h + 1) * DIM] = total[h:h + 1]
    next_on = seg_col == next_seg
    for h in range(heads):
        next_ref[h] = jnp.where(next_on, next_ref[h], 0.0)
    for d in (0, 1, 3, 2):
        h, cut = next_head(1, d)
        weight = next_ref[h]
        grad = split(state_in[1, h])
        dk = dk_acc[h] + weight * mm_split_right(v_ref[:, cut], grad, 1, 1)
        dv = dv_acc[h] + weight * mm_split_right(k_ref[:, cut], grad, 1, 0)
        dk_ref[:, cut] = dk.astype(BF16)
        dv_ref[:, cut] = dv.astype(BF16)
    sent(meta.at[row_others], meta_s.at[0])
    @pl.when(core == 0)
    def _():
        sent(states, a2a_s.at[0])

    @pl.when(core == 1)
    def _():
        sent(states.at[:, pl.ds(0, CHIPS - 1)], a2a_s.at[0])
        sent(prefixes.at[:, row_others], ret_s.at[0])
        moved = jnp.minimum(row, 2) + jnp.minimum(rows - 1 - row, 2)
        for n in (2, 3, 4):
            @pl.when(moved == n)
            def _():
                sent(carried.at[pl.ds(0, n)], col_s.at[0])

    @pl.when(pos == 1)
    def _():
        sent(edge, edge_s.at[0])

    if zs > 1:
        sent(z_all.at[pl.ds(0, zs - 1)], z_s.at[0])
    sent(gr_all.at[row_others], gr_s.at[0])
    sent(gc_all.at[pl.ds(0, rows - 1)], gc_s.at[0])


def store(*refs):
    count = (len(refs) - 1) // 2
    copies = [
        pltpu.make_async_copy(refs[i], refs[count + i], refs[-1].at[i]) for i in range(count)
    ]
    for copy in copies:
        copy.start()
    for copy in copies:
        copy.wait()


def local(queries, key_rows, value_rows, segment_ids, decay_span, norm_gain, out_grad):
    rows = lax.axis_size("seq") // ROW
    zs = lax.axis_size("head")
    heads = decay_span.shape[0]
    width = heads * DIM
    far = pl.BlockSpec(memory_space=pl.ANY)
    near = pl.BlockSpec(memory_space=pltpu.VMEM)
    wide = pltpu.VMEM((BLOCK, width), BF16)
    square = pltpu.VMEM((heads, DIM, DIM), F32)
    pieces = pltpu.VMEM((2, ROW, DIM, DIM), F32)
    per_head = pltpu.VMEM((2, heads, DIM, DIM), F32)
    dma = pltpu.SemaphoreType.DMA
    kept = pltpu.VMEM((1, width), F32)
    results = pl.pallas_call(
        functools.partial(kernel, rows, zs, heads),
        out_shape=(wide, wide, wide, kept),
        in_specs=[far] * 7,
        out_specs=(near,) * 4,
        scratch_shapes=[
            wide, wide, wide, wide,
            pltpu.VMEM((1, BLOCK), jnp.int32), pltpu.SMEM((heads,), F32), kept,
            pltpu.VMEM((2, DIM), F32),
            pltpu.VMEM((ROW, 2, DIM), F32),
            per_head,
            pieces,
            pltpu.VMEM((2, HEAD_ROWS + DIM, DIM), F32),
            pltpu.VMEM((4, HEAD_ROWS + DIM, DIM), F32),
            pieces,
            per_head,
            pltpu.VMEM((2, DIM), F32),
            pltpu.VMEM((zs, 2, DIM), F32),
            pltpu.VMEM((heads, DIM), F32),
            pltpu.VMEM((ROW, heads, DIM), F32),
            pltpu.VMEM((heads, DIM), F32),
            pltpu.VMEM((rows, heads, DIM), F32),
            square, square, square, square, square,
            pltpu.VMEM((heads, 2, DIM, DIM), BF16),
            dma((7,)),
            dma((1,)), dma((1,)),
            dma((1,)), dma((CHUNKS,)),
            dma((1,)), dma((2, CHUNKS)),
            dma((1,)), dma((CHIPS,)),
            dma((1,)), dma((1,)),
            dma((1,)), dma((1,)),
            dma((1,)), dma((1,)),
            pltpu.SemaphoreType.REGULAR((2, 2)),
            pltpu.VMEM((HEAD_ROWS, DIM), F32), dma((1,)), dma((1,)),
            square, square, square, square, square, square,
            pltpu.VMEM((heads, DIM, DIM), BF16),
        ],
        compiler_params=pltpu.CompilerParams(collective_id=0, has_side_effects=True),
    )(
        queries, key_rows, value_rows, out_grad,
        segment_ids.reshape(1, BLOCK), decay_span, norm_gain.reshape(1, width),
    )
    out = jax.ShapeDtypeStruct((BLOCK, width), BF16)
    dq, dk, dv, gg = pl.pallas_call(
        store,
        out_shape=(out, out, out, jax.ShapeDtypeStruct((1, width), F32)),
        in_specs=[near] * 4,
        out_specs=(far,) * 4,
        scratch_shapes=[dma((4,))],
    )(*[pltpu.with_memory_space_constraint(r, pltpu.VMEM) for r in results])
    return dq, dk, dv, gg.reshape(width)


def solution(mesh):
    in_specs = (
        P("seq", "head"),
        P("seq", "head"),
        P("seq", "head"),
        P("seq"),
        P("head"),
        P("head"),
        P("seq", "head"),
    )
    out_specs = (P("seq", "head"), P("seq", "head"), P("seq", "head"), P("head"))
    return jax.shard_map(local, mesh=mesh, in_specs=in_specs, out_specs=out_specs, check_vma=False)
```

```python
import functools

import jax
import jax.numpy as jnp
from jax import lax
from jax.experimental import pallas as pl
from jax.experimental.pallas import tpu as pltpu
from jax.sharding import PartitionSpec as P

DIM = 128
ROW = 8
BLOCK = 128
CHIPS = ROW // 2
CHUNKS = 8
PART = DIM // CHUNKS
HEAD_ROWS = 8
MESH = pl.DeviceIdType.MESH
F32 = jnp.float32
BF16 = jnp.bfloat16
ORDER = (4, 3, 5, 2, 6, 1, 7)


def split(x):
    high = x.astype(BF16)
    return high, (x - high.astype(F32)).astype(BF16)


def mm(a, b, ca, cb):
    return lax.dot_general(a, b, (((ca,), (cb,)), ((), ())), preferred_element_type=F32)


def mm_split_left(a, b, ca, cb):
    return mm(a[0], b, ca, cb) + mm(a[1], b, ca, cb)


def mm_split_right(a, b, ca, cb):
    return mm(a, b[0], ca, cb) + mm(a, b[1], ca, cb)


def mm_split_both(a, b, ca, cb):
    return mm(a[0], b[0], ca, cb) + (mm(a[0], b[1], ca, cb) + mm(a[1], b[0], ca, cb))


def kernel(
    rows, zs, heads,
    q_hbm, k_hbm, v_hbm, dy_hbm, seg_hbm, span_hbm, gain_hbm,
    dq_ref, dk_ref, dv_ref, gg_ref,
    q_ref, k_ref, v_ref, dy_ref, seg_ref, span_ref, gain_ref,
    meta_own, meta, states, gathered, totals, carried, prefixes, state_in,
    z_own, z_all, gr_own, gr_all, gc_own, gc_all,
    att_ref, back_ref, w_ref, dk_acc, dv_acc, qk_ref,
    in_sem, meta_s, meta_r, a2a_s, a2a_r, col_s, col_r, ret_s, ret_r,
    z_s, z_r, gr_s, gr_r, gc_s, gc_r, tokens, edge, edge_s, edge_r,
    into_ref, next_ref, start_ref, gdy_ref, start_gdy, start_att, q_turned,
    pair, landed, lam_ref, pair_s, pair_r, pass_s,
):
    me = lax.axis_index("seq")
    z = lax.axis_index("head")
    row = me // ROW
    pos = lax.rem(me, ROW)
    chip, core = pos // 2, lax.rem(pos, 2)
    features = float(zs * heads * DIM)

    loads = [
        pltpu.make_async_copy(src, dst, in_sem.at[i])
        for i, (src, dst) in enumerate(
            (
                (k_hbm, k_ref), (v_hbm, v_ref), (q_hbm, q_ref), (dy_hbm, dy_ref),
                (seg_hbm, seg_ref), (span_hbm, span_ref), (gain_hbm, gain_ref),
            )
        )
    ]
    for i in (4, 5, 0, 1, 2, 3, 6):
        loads[i].start()

    def seq_of(r, p):
        return {"seq": r * ROW + p, "head": z}

    row_mates = [lax.rem(pos + s, ROW) for s in ORDER]
    col_mates = [lax.rem(row + s, rows) for s in range(1, rows)]
    z_mates = [lax.rem(z + s, zs) for s in sorted(range(1, zs), key=lambda s: -min(s, zs - s))]
    z_sides = sorted({1 % zs, (zs - 1) % zs} - {0})
    up, down = row < rows - 1, row > 0
    y_sides = ((up, row + 1), (down, row - 1))
    barrier = pltpu.get_barrier_semaphore()
    for p in row_mates:
        pl.semaphore_signal(barrier, inc=1, device_id=seq_of(row, p), device_id_type=MESH)
    for s in z_sides:
        other = {"seq": me, "head": lax.rem(z + s, zs)}
        pl.semaphore_signal(barrier, inc=1, device_id=other, device_id_type=MESH)
    for near, other in y_sides:
        @pl.when(near)
        def _():
            pl.semaphore_signal(barrier, inc=1, device_id=seq_of(other, pos), device_id_type=MESH)

    y_waves, z_waves = rows - 2, zs // 2 - 1

    def token(wave):
        if wave < z_waves:
            for i, s in enumerate(z_sides):
                pl.semaphore_signal(
                    tokens.at[1, i], inc=1, device_id_type=MESH,
                    device_id={"seq": me, "head": lax.rem(z + s, zs)},
                )
        if wave < y_waves:
            for i, (near, other) in enumerate(y_sides):
                @pl.when(near)
                def _():
                    pl.semaphore_signal(
                        tokens.at[0, i], inc=1, device_id_type=MESH,
                        device_id=seq_of(other, pos),
                    )

    def take(wave):
        if wave < z_waves:
            for i in range(len(z_sides)):
                pl.semaphore_wait(tokens.at[1, i], 1)
        if wave < y_waves:
            for i, near in enumerate((down, up)):
                @pl.when(near)
                def _():
                    pl.semaphore_wait(tokens.at[0, i], 1)

    def step_tokens(wave):
        take(wave)
        token(wave + 1)

    def remote(src, dst, ss, rs, target):
        return pltpu.make_async_remote_copy(
            src_ref=src, dst_ref=dst, send_sem=ss, recv_sem=rs,
            device_id=target, device_id_type=MESH,
        )

    def send(*args):
        remote(*args).start()

    def arrived(buffer, rs):
        remote(buffer, buffer, rs, rs, seq_of(row, row_mates[0])).wait_recv()

    def sent(buffer, ss):
        remote(buffer, buffer, ss, ss, seq_of(row, row_mates[0])).wait_send()

    row_others = pl.ds(0, ROW - 1)
    loads[4].wait()
    loads[5].wait()

    t_col = lax.broadcasted_iota(jnp.int32, (BLOCK, DIM), 0).astype(F32)
    s_row = lax.broadcasted_iota(jnp.int32, (BLOCK, DIM), 1).astype(F32)
    seg_row = seg_ref[...].astype(F32)
    seg_tile = jnp.broadcast_to(seg_row, (BLOCK, DIM))
    seg_col = seg_tile.T
    first_own = jnp.broadcast_to(seg_row[:, 0:1], (1, DIM))
    last_own = jnp.broadcast_to(seg_row[:, BLOCK - 1:BLOCK], (1, DIM))
    meta_own[0:1] = last_own
    meta_own[1:2] = first_own
    meta[pos] = meta_own[...]

    inverse = [1.0 / jnp.full((1, DIM), span_ref[h], F32) for h in range(heads)]
    own_inverse = 1.0 / jnp.full((1, DIM), span_ref[chip], F32)
    lam = jnp.exp(-float(BLOCK) * own_inverse)
    for h in range(heads):
        lam_ref[h:h + 1] = jnp.exp(-float(BLOCK) * inverse[h])
    lam_row = jnp.exp(-float(BLOCK * ROW) * own_inverse)

    for h in range(heads):
        att_ref[h] = jnp.where(
            seg_col == last_own, jnp.exp((t_col - (BLOCK - 1.0)) * inverse[h]), 0.0
        )
    loads[0].wait()
    loads[1].wait()
    for h in range(heads):
        cut = slice(h * DIM, (h + 1) * DIM)
        local = mm_split_right(
            k_ref[:, cut], split(v_ref[:, cut].astype(F32) * att_ref[h]), 0, 0
        )
        states[0, h] = local

    pl.semaphore_wait(
        barrier, len(row_mates) + len(z_sides) + up.astype(jnp.int32) + down.astype(jnp.int32)
    )

    def scatter(side):
        for c in range(CHUNKS):
            part = pl.ds(c * PART, PART)
            for d in (2, 1, 3):
                h = lax.rem(chip + d, CHIPS)
                send(
                    states.at[side, h, part], gathered.at[side, pos, part],
                    a2a_s.at[0], a2a_r.at[c], seq_of(row, 2 * h + 1),
                )

            @pl.when(core == 0)
            def _():
                send(
                    states.at[side, chip, part], gathered.at[side, pos, part],
                    a2a_s.at[0], a2a_r.at[c], seq_of(row, pos + 1),
                )

        if side == 0:
            @pl.when(core == 0)
            def _():
                send(states.at[0], pair, pair_s.at[0], pair_r.at[0], seq_of(row, pos + 1))

        @pl.when(core == 1)
        def _():
            gathered[side, pos] = states[side, chip]

    def piece(c):
        return pl.ds(HEAD_ROWS + c * PART, PART) if c else pl.ds(0, HEAD_ROWS + PART)

    def order_of(side):
        order = list(range(ROW)) if side == 0 else list(range(ROW - 1, -1, -1))
        return order, [meta[a, side:side + 1, :] for a in order]

    for p in row_mates:
        send(meta_own, meta.at[pos], meta_s.at[0], meta_r.at[0], seq_of(row, p))
    scatter(0)

    def before_of(side):
        return row if side == 0 else rows - 1 - row

    def after_of(side):
        return rows - 1 - row if side == 0 else row

    token(0)
    for side in range(2):
        for step in range(2):
            @pl.when(before_of(side) <= step)
            def _():
                carried[2 * side + step, :HEAD_ROWS] = jnp.full((HEAD_ROWS, DIM), -1.0, F32)
                carried[2 * side + step, HEAD_ROWS:] = jnp.zeros((DIM, DIM), F32)

    def scan_first(side):
        order, seg_of = order_of(side)
        factor = [jnp.where(seg_of[n] == seg_of[n - 1], lam, 0.0) for n in range(1, ROW)]
        for c in range(CHUNKS):
            part = pl.ds(c * PART, PART)
            arrived(gathered.at[side, row_others, part], a2a_r.at[c])
            run = gathered[side, order[0], part]
            for n in range(1, ROW):
                run = gathered[side, order[n], part] + factor[n - 1] * run
            if c == 0:
                totals[side, :HEAD_ROWS] = jnp.broadcast_to(seg_of[-1], (HEAD_ROWS, DIM))
            totals[side, pl.ds(HEAD_ROWS + c * PART, PART)] = run
            for step in (1, 0):
                @pl.when(after_of(side) > step)
                def _():
                    send(
                        totals.at[side, piece(c)], carried.at[2 * side + step, piece(c)],
                        col_s.at[0], col_r.at[side, c],
                        seq_of(row + (step + 1 if side == 0 else -step - 1), pos),
                    )

    def scan_second(side):
        order, seg_of = order_of(side)
        for c in range(CHUNKS):
            @pl.when(before_of(side) == 1)
            def _():
                arrived(carried.at[2 * side, piece(c)], col_r.at[side, c])

            @pl.when(before_of(side) > 1)
            def _():
                arrived(carried.at[pl.ds(2 * side, 2), piece(c)], col_r.at[side, c])

            if c == 0:
                if side == 0:
                    @pl.when(pos == 1)
                    def _():
                        send(carried.at[0, pl.ds(0, HEAD_ROWS)], edge,
                             edge_s.at[0], edge_r.at[0], seq_of(row, pos - 1))
                near_seg = carried[2 * side, 0:1]
                far_seg = carried[2 * side + 1, 0:1]
                far_on = jnp.where(far_seg == near_seg, lam_row, 0.0)
                prev = [near_seg] + seg_of[:-1]
                factor = [jnp.where(a == b, lam, 0.0) for a, b in zip(seg_of, prev)]
            rows_c = pl.ds(HEAD_ROWS + c * PART, PART)
            part = pl.ds(c * PART, PART)
            run = carried[2 * side, rows_c] + far_on * carried[2 * side + 1, rows_c]
            for n in range(ROW):
                if side or order[n] % 2 == 0:
                    prefixes[side, order[n], part] = run
                if n < ROW - 1:
                    run = gathered[side, order[n], part] + factor[n] * run
            if side:
                for p in row_mates:
                    send(
                        prefixes.at[1, p, part], state_in.at[1, chip, part], ret_s.at[0],
                        ret_r.at[lax.rem(chip + CHIPS - p // 2, CHIPS)], seq_of(row, p),
                    )
            else:
                for d in (2, 1, 3):
                    t = lax.rem(chip + d, CHIPS)
                    send(
                        prefixes.at[0, 2 * t, part], landed.at[chip, part],
                        ret_s.at[0], ret_r.at[CHIPS - d], seq_of(row, 2 * t + 1),
                    )
        if side:
            state_in[1, chip] = prefixes[1, pos]
        else:
            landed[chip] = prefixes[0, 2 * chip]

    def next_head(side, d):
        head = lax.rem(chip + d, CHIPS)

        @pl.when(core == 0)
        def _():
            arrived(state_in.at[side, head], ret_r.at[d])

        @pl.when(core == 1)
        def _():
            if side:
                if d:
                    arrived(state_in.at[1, head], ret_r.at[d])
            else:
                if d:
                    arrived(landed.at[head], ret_r.at[d])
                send(
                    landed.at[head], state_in.at[0, head],
                    pass_s.at[0], ret_r.at[d], seq_of(row, pos - 1),
                )
                before = jnp.where(chip == 0, carried[0, 0:1], meta[lax.rem(pos + ROW - 2, ROW), 0:1, :])
                factor = jnp.where(meta[pos - 1, 0:1, :] == before, lam_ref[pl.ds(head, 1)], 0.0)
                state_in[0, head] = pair[head] + factor * landed[head]
        return head, pl.ds(pl.multiple_of(head * DIM, DIM), DIM)

    loads[2].wait()
    causal = t_col >= s_row
    same = seg_col == seg_tile
    keep = jnp.logical_and(causal, same)
    for h in range(heads):
        cut = slice(h * DIM, (h + 1) * DIM)
        weights = jnp.where(keep, jnp.exp(jnp.minimum(s_row - t_col, 0.0) * inverse[h]), 0.0)
        w_ref[h] = weights
        scores = split(mm(q_ref[:, cut], k_ref[:, cut], 1, 1) * weights)
        qk_ref[h, 0] = scores[0]
        qk_ref[h, 1] = scores[1]
        att_ref[h] = mm_split_left(scores, v_ref[:, cut], 1, 0)
        into_ref[h] = jnp.exp(-(t_col + 1.0) * inverse[h])
        next_ref[h] = jnp.exp((t_col - float(BLOCK)) * inverse[h])
        start_ref[h] = jnp.where(seg_col == first_own, jnp.exp(-t_col * inverse[h]), 0.0)

    loads[3].wait()
    loads[6].wait()
    for h in range(heads):
        cut = slice(h * DIM, (h + 1) * DIM)
        gdy_ref[h] = gain_ref[:, cut] * dy_ref[:, cut].astype(F32)
    step_tokens(0)
    arrived(meta.at[row_others], meta_r.at[0])
    pl.when(core == 1)(lambda: scan_first(0))
    step_tokens(1)
    pl.when(core == 1)(lambda: scan_second(0))
    step_tokens(2)
    step_tokens(3)

    @pl.when(pos == 0)
    def _():
        arrived(edge, edge_r.at[0])

    prev_seg = jnp.where(pos == 0, edge[0:1], meta[lax.rem(pos + ROW - 1, ROW), 0:1, :])
    into_on = seg_col == prev_seg
    for h in range(heads):
        into_ref[h] = jnp.where(into_on, into_ref[h], 0.0)
    @pl.when(core == 1)
    def _():
        arrived(pair, pair_r.at[0])

    squares = jnp.zeros((BLOCK, DIM), F32)
    crosses = jnp.zeros((BLOCK, DIM), F32)
    for d in (0, 1, 3, 2):
        h, cut = next_head(0, d)
        state = split(state_in[0, h])
        att = att_ref[h] + into_ref[h] * mm_split_right(q_ref[:, cut], state, 1, 0)
        att_ref[h] = att
        squares = squares + att * att
        crosses = crosses + gdy_ref[h] * att
    square_row = jnp.sum(squares.T, axis=0, keepdims=True)
    cross_row = jnp.sum(crosses.T, axis=0, keepdims=True)
    z_own[0:1] = square_row
    z_own[1:2] = cross_row
    for other in z_mates:
        send(z_own, z_all.at[z], z_s.at[0], z_r.at[0], {"seq": me, "head": other})
    z_all[z] = z_own[...]
    step_tokens(4)
    for h in range(heads):
        start_gdy[h] = start_ref[h] * gdy_ref[h]
        start_att[h] = start_ref[h] * att_ref[h]
        q_turned[h] = q_ref[:, h * DIM:(h + 1) * DIM].T
    if zs > 1:
        arrived(z_all.at[pl.ds(0, zs - 1)], z_r.at[0])
    both = z_all[0]
    for i in range(1, zs):
        both = both + z_all[i]
    inv_row = lax.rsqrt(both[0:1] / features + 1e-06)
    off_row = inv_row * inv_row * inv_row * both[1:2] / features
    inv = jnp.broadcast_to(inv_row, (BLOCK, DIM)).T
    off = jnp.broadcast_to(off_row, (BLOCK, DIM)).T

    for h in range(heads):
        scaled = split(inv * start_gdy[h] - off * start_att[h])
        states[1, h] = mm_split_right(q_turned[h], scaled, 1, 0)
    scatter(1)
    for h in range(heads):
        cut = slice(h * DIM, (h + 1) * DIM)
        att = att_ref[h]
        back_ref[h] = gdy_ref[h] * inv - att * off
        gc_own[h:h + 1] = jnp.sum(dy_ref[:, cut].astype(F32) * inv * att, axis=0, keepdims=True)
    step_tokens(5)
    for r in col_mates:
        send(gc_own, gc_all.at[row], gc_s.at[0], gc_r.at[0], seq_of(r, pos))
    gc_all[row] = gc_own[...]

    def inner(h):
        cut = slice(h * DIM, (h + 1) * DIM)
        back = split(back_ref[h])
        weights = w_ref[h]
        grads = split(mm_split_left(back, v_ref[:, cut], 1, 1) * weights)
        into = into_ref[h]
        state = split(state_in[0, h])
        dq = mm_split_left(grads, k_ref[:, cut], 1, 0) + into * mm_split_both(back, state, 1, 1)
        dq_ref[:, cut] = dq.astype(BF16)
        dk_acc[h] = mm_split_left(grads, q_ref[:, cut], 0, 0)
        dv_acc[h] = mm_split_both((qk_ref[h, 0], qk_ref[h, 1]), back, 0, 0)

    inner(0)
    inner(1)
    pl.when(core == 1)(lambda: scan_first(1))
    inner(2)
    pl.when(core == 1)(lambda: scan_second(1))
    next_seg = jnp.where(
        pos == ROW - 1, carried[2, 0:1], meta[lax.rem(pos + 1, ROW), 1:2, :]
    )
    inner(3)
    arrived(gc_all.at[pl.ds(0, rows - 1)], gc_r.at[0])
    total = gc_all[0]
    for a in range(1, rows):
        total = total + gc_all[a]
    gr_own[...] = total
    gr_all[pos] = total
    for p in row_mates:
        send(gr_own, gr_all.at[pos], gr_s.at[0], gr_r.at[0], seq_of(row, p))

    next_on = seg_col == next_seg
    for h in range(heads):
        next_ref[h] = jnp.where(next_on, next_ref[h], 0.0)
    for d in (0, 1, 3, 2):
        h, cut = next_head(1, d)
        weight = next_ref[h]
        grad = split(state_in[1, h])
        dk = dk_acc[h] + weight * mm_split_right(v_ref[:, cut], grad, 1, 1)
        dv = dv_acc[h] + weight * mm_split_right(k_ref[:, cut], grad, 1, 0)
        dk_ref[:, cut] = dk.astype(BF16)
        dv_ref[:, cut] = dv.astype(BF16)
    arrived(gr_all.at[row_others], gr_r.at[0])
    total = gr_all[0]
    for a in range(1, ROW):
        total = total + gr_all[a]
    for h in range(heads):
        gg_ref[:, h * DIM:(h + 1) * DIM] = total[h:h + 1]
    sent(meta.at[row_others], meta_s.at[0])
    @pl.when(core == 0)
    def _():
        sent(states, a2a_s.at[0])
        sent(pair, pair_s.at[0])

    @pl.when(core == 1)
    def _():
        sent(states.at[:, pl.ds(0, CHIPS - 1)], a2a_s.at[0])
        sent(prefixes.at[:, pl.ds(0, 5)], ret_s.at[0])
        sent(landed, pass_s.at[0])
        moved = jnp.minimum(row, 2) + jnp.minimum(rows - 1 - row, 2)
        for n in (2, 3, 4):
            @pl.when(moved == n)
            def _():
                sent(carried.at[pl.ds(0, n)], col_s.at[0])

    @pl.when(pos == 1)
    def _():
        sent(edge, edge_s.at[0])

    if zs > 1:
        sent(z_all.at[pl.ds(0, zs - 1)], z_s.at[0])
    sent(gr_all.at[row_others], gr_s.at[0])
    sent(gc_all.at[pl.ds(0, rows - 1)], gc_s.at[0])


def store(*refs):
    count = (len(refs) - 1) // 2
    copies = [
        pltpu.make_async_copy(refs[i], refs[count + i], refs[-1].at[i]) for i in range(count)
    ]
    for copy in copies:
        copy.start()
    for copy in copies:
        copy.wait()


def local(queries, key_rows, value_rows, segment_ids, decay_span, norm_gain, out_grad):
    rows = lax.axis_size("seq") // ROW
    zs = lax.axis_size("head")
    heads = decay_span.shape[0]
    width = heads * DIM
    far = pl.BlockSpec(memory_space=pl.ANY)
    near = pl.BlockSpec(memory_space=pltpu.VMEM)
    wide = pltpu.VMEM((BLOCK, width), BF16)
    square = pltpu.VMEM((heads, DIM, DIM), F32)
    pieces = pltpu.VMEM((2, ROW, DIM, DIM), F32)
    per_head = pltpu.VMEM((2, heads, DIM, DIM), F32)
    dma = pltpu.SemaphoreType.DMA
    kept = pltpu.VMEM((1, width), F32)
    results = pl.pallas_call(
        functools.partial(kernel, rows, zs, heads),
        out_shape=(wide, wide, wide, kept),
        in_specs=[far] * 7,
        out_specs=(near,) * 4,
        scratch_shapes=[
            wide, wide, wide, wide,
            pltpu.VMEM((1, BLOCK), jnp.int32), pltpu.SMEM((heads,), F32), kept,
            pltpu.VMEM((2, DIM), F32),
            pltpu.VMEM((ROW, 2, DIM), F32),
            per_head,
            pieces,
            pltpu.VMEM((2, HEAD_ROWS + DIM, DIM), F32),
            pltpu.VMEM((4, HEAD_ROWS + DIM, DIM), F32),
            pieces,
            per_head,
            pltpu.VMEM((2, DIM), F32),
            pltpu.VMEM((zs, 2, DIM), F32),
            pltpu.VMEM((heads, DIM), F32),
            pltpu.VMEM((ROW, heads, DIM), F32),
            pltpu.VMEM((heads, DIM), F32),
            pltpu.VMEM((rows, heads, DIM), F32),
            square, square, square, square, square,
            pltpu.VMEM((heads, 2, DIM, DIM), BF16),
            dma((7,)),
            dma((1,)), dma((1,)),
            dma((1,)), dma((CHUNKS,)),
            dma((1,)), dma((2, CHUNKS)),
            dma((1,)), dma((CHIPS,)),
            dma((1,)), dma((1,)),
            dma((1,)), dma((1,)),
            dma((1,)), dma((1,)),
            pltpu.SemaphoreType.REGULAR((2, 2)),
            pltpu.VMEM((HEAD_ROWS, DIM), F32), dma((1,)), dma((1,)),
            square, square, square, square, square, square,
            pltpu.VMEM((heads, DIM, DIM), BF16),
            square, square, pltpu.VMEM((heads, DIM), F32),
            dma((1,)), dma((1,)), dma((1,)),
        ],
        compiler_params=pltpu.CompilerParams(collective_id=0, has_side_effects=True),
    )(
        queries, key_rows, value_rows, out_grad,
        segment_ids.reshape(1, BLOCK), decay_span, norm_gain.reshape(1, width),
    )
    out = jax.ShapeDtypeStruct((BLOCK, width), BF16)
    dq, dk, dv, gg = pl.pallas_call(
        store,
        out_shape=(out, out, out, jax.ShapeDtypeStruct((1, width), F32)),
        in_specs=[near] * 4,
        out_specs=(far,) * 4,
        scratch_shapes=[dma((4,))],
    )(*[pltpu.with_memory_space_constraint(r, pltpu.VMEM) for r in results])
    return dq, dk, dv, gg.reshape(width)


def solution(mesh):
    in_specs = (
        P("seq", "head"),
        P("seq", "head"),
        P("seq", "head"),
        P("seq"),
        P("head"),
        P("head"),
        P("seq", "head"),
    )
    out_specs = (P("seq", "head"), P("seq", "head"), P("seq", "head"), P("head"))
    return jax.shard_map(local, mesh=mesh, in_specs=in_specs, out_specs=out_specs, check_vma=False)
```

```python
import functools

import jax
import jax.numpy as jnp
from jax import lax
from jax.experimental import pallas as pl
from jax.experimental.pallas import tpu as pltpu
from jax.sharding import PartitionSpec as P

DIM = 128
ROW = 8
BLOCK = 128
CHIPS = ROW // 2
CHUNKS = 8
PART = DIM // CHUNKS
HEAD_ROWS = 8
MESH = pl.DeviceIdType.MESH
F32 = jnp.float32
BF16 = jnp.bfloat16
ORDER = (4, 3, 5, 2, 6, 1, 7)


def split(x):
    high = x.astype(BF16)
    return high, (x - high.astype(F32)).astype(BF16)


def mm(a, b, ca, cb):
    return lax.dot_general(a, b, (((ca,), (cb,)), ((), ())), preferred_element_type=F32)


def mm_split_left(a, b, ca, cb):
    return mm(a[0], b, ca, cb) + mm(a[1], b, ca, cb)


def mm_split_right(a, b, ca, cb):
    return mm(a, b[0], ca, cb) + mm(a, b[1], ca, cb)


def mm_split_both(a, b, ca, cb):
    return mm(a[0], b[0], ca, cb) + (mm(a[0], b[1], ca, cb) + mm(a[1], b[0], ca, cb))


def kernel(
    rows, zs, heads,
    q_hbm, k_hbm, v_hbm, dy_hbm, seg_hbm, span_hbm, gain_hbm,
    dq_ref, dk_ref, dv_ref, gg_ref,
    kv_ref, qd_ref, seg_ref, span_ref, gain_ref,
    meta_own, meta, states, gathered, totals, carried, prefixes, state_in,
    z_own, z_all, gr_own, gr_all, gc_own, gc_all,
    att_ref, back_ref, w_ref, dk_acc, dv_acc, qk_ref,
    in_sem, small_s, meta_r, a2a_s, a2a_r, col_s, col_r, ret_s, ret_r,
    z_r, gr_r, gc_r, tokens, edge, edge_r,
    into_ref, next_ref, start_ref, gdy_ref, start_gdy, start_att, q_turned,
    pair, landed, lam_ref, pair_s, pair_r, pass_s,
):
    me = lax.axis_index("seq")
    z = lax.axis_index("head")
    row = me // ROW
    pos = lax.rem(me, ROW)
    chip, core = pos // 2, lax.rem(pos, 2)
    features = float(zs * heads * DIM)
    k_ref, v_ref, q_ref, dy_ref = kv_ref.at[0], kv_ref.at[1], qd_ref.at[0], qd_ref.at[1]

    def load(src, dst, i):
        return pltpu.make_async_copy(src, dst, in_sem.at[i])

    for src, dst, i in (
        (seg_hbm, seg_ref, 2), (span_hbm, span_ref, 3), (k_hbm, k_ref, 0), (v_hbm, v_ref, 0),
        (q_hbm, q_ref, 1), (dy_hbm, dy_ref, 1), (gain_hbm, gain_ref, 4),
    ):
        load(src, dst, i).start()

    def seq_of(r, p):
        return {"seq": r * ROW + p, "head": z}

    row_mates = [lax.rem(pos + s, ROW) for s in ORDER]
    col_mates = [lax.rem(row + s, rows) for s in range(1, rows)]
    z_mates = [lax.rem(z + s, zs) for s in sorted(range(1, zs), key=lambda s: -min(s, zs - s))]
    z_sides = sorted({1 % zs, (zs - 1) % zs} - {0})
    up, down = row < rows - 1, row > 0
    y_sides = ((up, row + 1), (down, row - 1))
    barrier = pltpu.get_barrier_semaphore()
    for p in row_mates:
        pl.semaphore_signal(barrier, inc=1, device_id=seq_of(row, p), device_id_type=MESH)
    for s in z_sides:
        other = {"seq": me, "head": lax.rem(z + s, zs)}
        pl.semaphore_signal(barrier, inc=1, device_id=other, device_id_type=MESH)
    for near, other in y_sides:
        @pl.when(near)
        def _():
            pl.semaphore_signal(barrier, inc=1, device_id=seq_of(other, pos), device_id_type=MESH)

    y_waves, z_waves = rows - 2, zs // 2 - 1

    def token(wave):
        if wave < z_waves:
            for i, s in enumerate(z_sides):
                pl.semaphore_signal(
                    tokens.at[1, i], inc=1, device_id_type=MESH,
                    device_id={"seq": me, "head": lax.rem(z + s, zs)},
                )
        if wave < y_waves:
            for i, (near, other) in enumerate(y_sides):
                @pl.when(near)
                def _():
                    pl.semaphore_signal(
                        tokens.at[0, i], inc=1, device_id_type=MESH,
                        device_id=seq_of(other, pos),
                    )

    def take(wave):
        if wave < z_waves:
            for i in range(len(z_sides)):
                pl.semaphore_wait(tokens.at[1, i], 1)
        if wave < y_waves:
            for i, near in enumerate((down, up)):
                @pl.when(near)
                def _():
                    pl.semaphore_wait(tokens.at[0, i], 1)

    def step_tokens(wave):
        take(wave)
        token(wave + 1)

    def remote(src, dst, ss, rs, target):
        return pltpu.make_async_remote_copy(
            src_ref=src, dst_ref=dst, send_sem=ss, recv_sem=rs,
            device_id=target, device_id_type=MESH,
        )

    def send(*args):
        remote(*args).start()

    def arrived(buffer, rs):
        remote(buffer, buffer, rs, rs, seq_of(row, row_mates[0])).wait_recv()

    def sent(buffer, ss):
        remote(buffer, buffer, ss, ss, seq_of(row, row_mates[0])).wait_send()

    row_others = pl.ds(0, ROW - 1)
    load(seg_hbm, seg_ref, 2).wait()
    load(span_hbm, span_ref, 3).wait()

    t_col = lax.broadcasted_iota(jnp.int32, (BLOCK, DIM), 0).astype(F32)
    s_row = lax.broadcasted_iota(jnp.int32, (BLOCK, DIM), 1).astype(F32)
    seg_row = seg_ref[...].astype(F32)
    seg_tile = jnp.broadcast_to(seg_row, (BLOCK, DIM))
    seg_col = seg_tile.T
    first_own = jnp.broadcast_to(seg_row[:, 0:1], (1, DIM))
    last_own = jnp.broadcast_to(seg_row[:, BLOCK - 1:BLOCK], (1, DIM))
    meta_own[0:1] = last_own
    meta_own[1:2] = first_own
    meta[pos] = meta_own[...]

    inverse = [1.0 / jnp.full((1, DIM), span_ref[h], F32) for h in range(heads)]
    own_inverse = 1.0 / jnp.full((1, DIM), span_ref[chip], F32)
    lam = jnp.exp(-float(BLOCK) * own_inverse)
    for h in range(heads):
        lam_ref[h:h + 1] = jnp.exp(-float(BLOCK) * inverse[h])
    lam_row = jnp.exp(-float(BLOCK * ROW) * own_inverse)

    for h in range(heads):
        att_ref[h] = jnp.where(
            seg_col == last_own, jnp.exp((t_col - (BLOCK - 1.0)) * inverse[h]), 0.0
        )
    load(kv_ref, kv_ref, 0).wait()
    for h in range(heads):
        cut = slice(h * DIM, (h + 1) * DIM)
        local = mm_split_right(
            k_ref[:, cut], split(v_ref[:, cut].astype(F32) * att_ref[h]), 0, 0
        )
        states[0, h] = local

    pl.semaphore_wait(
        barrier, len(row_mates) + len(z_sides) + up.astype(jnp.int32) + down.astype(jnp.int32)
    )

    def scatter(side):
        for c in range(CHUNKS):
            part = pl.ds(c * PART, PART)
            for d in (2, 1, 3):
                h = lax.rem(chip + d, CHIPS)
                send(
                    states.at[side, h, part], gathered.at[side, pos, part],
                    a2a_s.at[0], a2a_r.at[c], seq_of(row, 2 * h + 1),
                )

            @pl.when(core == 0)
            def _():
                send(
                    states.at[side, chip, part], gathered.at[side, pos, part],
                    a2a_s.at[0], a2a_r.at[c], seq_of(row, pos + 1),
                )

        if side == 0:
            @pl.when(core == 0)
            def _():
                send(states.at[0], pair, pair_s.at[0], pair_r.at[0], seq_of(row, pos + 1))

        @pl.when(core == 1)
        def _():
            gathered[side, pos] = states[side, chip]

    def piece(c):
        return pl.ds(HEAD_ROWS + c * PART, PART) if c else pl.ds(0, HEAD_ROWS + PART)

    def order_of(side):
        order = list(range(ROW)) if side == 0 else list(range(ROW - 1, -1, -1))
        return order, [meta[a, side:side + 1, :] for a in order]

    for p in row_mates:
        send(meta_own, meta.at[pos], small_s.at[0], meta_r.at[0], seq_of(row, p))
    scatter(0)

    def before_of(side):
        return row if side == 0 else rows - 1 - row

    def after_of(side):
        return rows - 1 - row if side == 0 else row

    token(0)
    for side in range(2):
        for step in range(2):
            @pl.when(before_of(side) <= step)
            def _():
                carried[2 * side + step, :HEAD_ROWS] = jnp.full((HEAD_ROWS, DIM), -1.0, F32)
                carried[2 * side + step, HEAD_ROWS:] = jnp.zeros((DIM, DIM), F32)

    def scan_first(side):
        order, seg_of = order_of(side)
        factor = [jnp.where(seg_of[n] == seg_of[n - 1], lam, 0.0) for n in range(1, ROW)]
        for c in range(CHUNKS):
            part = pl.ds(c * PART, PART)
            arrived(gathered.at[side, row_others, part], a2a_r.at[c])
            run = gathered[side, order[0], part]
            for n in range(1, ROW):
                run = gathered[side, order[n], part] + factor[n - 1] * run
            if c == 0:
                totals[side, :HEAD_ROWS] = jnp.broadcast_to(seg_of[-1], (HEAD_ROWS, DIM))
            totals[side, pl.ds(HEAD_ROWS + c * PART, PART)] = run
            for step in (1, 0):
                @pl.when(after_of(side) > step)
                def _():
                    send(
                        totals.at[side, piece(c)], carried.at[2 * side + step, piece(c)],
                        col_s.at[0], col_r.at[side, c],
                        seq_of(row + (step + 1 if side == 0 else -step - 1), pos),
                    )

    def scan_second(side):
        order, seg_of = order_of(side)
        for c in range(CHUNKS):
            @pl.when(before_of(side) == 1)
            def _():
                arrived(carried.at[2 * side, piece(c)], col_r.at[side, c])

            @pl.when(before_of(side) > 1)
            def _():
                arrived(carried.at[pl.ds(2 * side, 2), piece(c)], col_r.at[side, c])

            if c == 0:
                if side == 0:
                    @pl.when(pos == 1)
                    def _():
                        send(carried.at[0, pl.ds(0, HEAD_ROWS)], edge,
                             small_s.at[0], edge_r.at[0], seq_of(row, pos - 1))
                near_seg = carried[2 * side, 0:1]
                far_seg = carried[2 * side + 1, 0:1]
                far_on = jnp.where(far_seg == near_seg, lam_row, 0.0)
                prev = [near_seg] + seg_of[:-1]
                factor = [jnp.where(a == b, lam, 0.0) for a, b in zip(seg_of, prev)]
            rows_c = pl.ds(HEAD_ROWS + c * PART, PART)
            part = pl.ds(c * PART, PART)
            run = carried[2 * side, rows_c] + far_on * carried[2 * side + 1, rows_c]
            for n in range(ROW):
                if side or order[n] % 2 == 0:
                    prefixes[side, order[n], part] = run
                if n < ROW - 1:
                    run = gathered[side, order[n], part] + factor[n] * run
            if side:
                for p in row_mates:
                    send(
                        prefixes.at[1, p, part], state_in.at[1, chip, part], ret_s.at[0],
                        ret_r.at[lax.rem(chip + CHIPS - p // 2, CHIPS)], seq_of(row, p),
                    )
            else:
                for d in (2, 1, 3):
                    t = lax.rem(chip + d, CHIPS)
                    send(
                        prefixes.at[0, 2 * t, part], landed.at[chip, part],
                        ret_s.at[0], ret_r.at[CHIPS - d], seq_of(row, 2 * t + 1),
                    )
        if side:
            state_in[1, chip] = prefixes[1, pos]
        else:
            landed[chip] = prefixes[0, 2 * chip]

    def next_head(side, d):
        head = lax.rem(chip + d, CHIPS)

        @pl.when(core == 0)
        def _():
            arrived(state_in.at[side, head], ret_r.at[d])

        @pl.when(core == 1)
        def _():
            if side:
                if d:
                    arrived(state_in.at[1, head], ret_r.at[d])
            else:
                if d:
                    arrived(landed.at[head], ret_r.at[d])
                send(
                    landed.at[head], state_in.at[0, head],
                    pass_s.at[0], ret_r.at[d], seq_of(row, pos - 1),
                )
                before = jnp.where(chip == 0, carried[0, 0:1], meta[lax.rem(pos + ROW - 2, ROW), 0:1, :])
                factor = jnp.where(meta[pos - 1, 0:1, :] == before, lam_ref[pl.ds(head, 1)], 0.0)
                state_in[0, head] = pair[head] + factor * landed[head]
        return head, pl.ds(pl.multiple_of(head * DIM, DIM), DIM)

    load(qd_ref, qd_ref, 1).wait()
    causal = t_col >= s_row
    same = seg_col == seg_tile
    keep = jnp.logical_and(causal, same)
    for h in range(heads):
        cut = slice(h * DIM, (h + 1) * DIM)
        weights = jnp.where(keep, jnp.exp(jnp.minimum(s_row - t_col, 0.0) * inverse[h]), 0.0)
        w_ref[h] = weights
        scores = split(mm(q_ref[:, cut], k_ref[:, cut], 1, 1) * weights)
        qk_ref[h, 0] = scores[0]
        qk_ref[h, 1] = scores[1]
        att_ref[h] = mm_split_left(scores, v_ref[:, cut], 1, 0)
        into_ref[h] = jnp.exp(-(t_col + 1.0) * inverse[h])
        next_ref[h] = jnp.exp((t_col - float(BLOCK)) * inverse[h])
        start_ref[h] = jnp.where(seg_col == first_own, jnp.exp(-t_col * inverse[h]), 0.0)

    load(gain_hbm, gain_ref, 4).wait()
    for h in range(heads):
        cut = slice(h * DIM, (h + 1) * DIM)
        gdy_ref[h] = gain_ref[:, cut] * dy_ref[:, cut].astype(F32)
    step_tokens(0)
    arrived(meta.at[row_others], meta_r.at[0])
    pl.when(core == 1)(lambda: scan_first(0))
    step_tokens(1)
    pl.when(core == 1)(lambda: scan_second(0))
    step_tokens(2)
    step_tokens(3)

    @pl.when(pos == 0)
    def _():
        arrived(edge, edge_r.at[0])

    prev_seg = jnp.where(pos == 0, edge[0:1], meta[lax.rem(pos + ROW - 1, ROW), 0:1, :])
    into_on = seg_col == prev_seg
    for h in range(heads):
        into_ref[h] = jnp.where(into_on, into_ref[h], 0.0)
    @pl.when(core == 1)
    def _():
        arrived(pair, pair_r.at[0])

    squares = jnp.zeros((BLOCK, DIM), F32)
    crosses = jnp.zeros((BLOCK, DIM), F32)
    for d in (0, 1, 3, 2):
        h, cut = next_head(0, d)
        state = split(state_in[0, h])
        att = att_ref[h] + into_ref[h] * mm_split_right(q_ref[:, cut], state, 1, 0)
        att_ref[h] = att
        squares = squares + att * att
        crosses = crosses + gdy_ref[h] * att
    square_row = jnp.sum(squares.T, axis=0, keepdims=True)
    cross_row = jnp.sum(crosses.T, axis=0, keepdims=True)
    z_own[0:1] = square_row
    z_own[1:2] = cross_row
    for other in z_mates:
        send(z_own, z_all.at[z], small_s.at[0], z_r.at[0], {"seq": me, "head": other})
    z_all[z] = z_own[...]
    step_tokens(4)
    for h in range(heads):
        start_gdy[h] = start_ref[h] * gdy_ref[h]
        start_att[h] = start_ref[h] * att_ref[h]
        q_turned[h] = q_ref[:, h * DIM:(h + 1) * DIM].T
    if zs > 1:
        arrived(z_all.at[pl.ds(0, zs - 1)], z_r.at[0])
    both = z_all[0]
    for i in range(1, zs):
        both = both + z_all[i]
    inv_row = lax.rsqrt(both[0:1] / features + 1e-06)
    off_row = inv_row * inv_row * inv_row * both[1:2] / features
    inv = jnp.broadcast_to(inv_row, (BLOCK, DIM)).T
    off = jnp.broadcast_to(off_row, (BLOCK, DIM)).T

    for h in range(heads):
        scaled = split(inv * start_gdy[h] - off * start_att[h])
        states[1, h] = mm_split_right(q_turned[h], scaled, 1, 0)
    scatter(1)
    for h in range(heads):
        cut = slice(h * DIM, (h + 1) * DIM)
        att = att_ref[h]
        back_ref[h] = gdy_ref[h] * inv - att * off
        gc_own[h:h + 1] = jnp.sum(dy_ref[:, cut].astype(F32) * inv * att, axis=0, keepdims=True)
    step_tokens(5)
    for r in col_mates:
        send(gc_own, gc_all.at[row], small_s.at[0], gc_r.at[0], seq_of(r, pos))
    gc_all[row] = gc_own[...]

    def inner(h):
        cut = slice(h * DIM, (h + 1) * DIM)
        back = split(back_ref[h])
        weights = w_ref[h]
        grads = split(mm_split_left(back, v_ref[:, cut], 1, 1) * weights)
        into = into_ref[h]
        state = split(state_in[0, h])
        dq = mm_split_left(grads, k_ref[:, cut], 1, 0) + into * mm_split_both(back, state, 1, 1)
        dq_ref[:, cut] = dq.astype(BF16)
        dk_acc[h] = mm_split_left(grads, q_ref[:, cut], 0, 0)
        dv_acc[h] = mm_split_both((qk_ref[h, 0], qk_ref[h, 1]), back, 0, 0)

    inner(0)
    inner(1)
    pl.when(core == 1)(lambda: scan_first(1))
    inner(2)
    pl.when(core == 1)(lambda: scan_second(1))
    next_seg = jnp.where(
        pos == ROW - 1, carried[2, 0:1], meta[lax.rem(pos + 1, ROW), 1:2, :]
    )
    inner(3)
    arrived(gc_all.at[pl.ds(0, rows - 1)], gc_r.at[0])
    total = gc_all[0]
    for a in range(1, rows):
        total = total + gc_all[a]
    gr_own[...] = total
    gr_all[pos] = total
    for p in row_mates:
        send(gr_own, gr_all.at[pos], small_s.at[0], gr_r.at[0], seq_of(row, p))

    next_on = seg_col == next_seg
    for h in range(heads):
        next_ref[h] = jnp.where(next_on, next_ref[h], 0.0)
    for d in (0, 1, 3, 2):
        h, cut = next_head(1, d)
        weight = next_ref[h]
        grad = split(state_in[1, h])
        dk = dk_acc[h] + weight * mm_split_right(v_ref[:, cut], grad, 1, 1)
        dv = dv_acc[h] + weight * mm_split_right(k_ref[:, cut], grad, 1, 0)
        dk_ref[:, cut] = dk.astype(BF16)
        dv_ref[:, cut] = dv.astype(BF16)
    arrived(gr_all.at[row_others], gr_r.at[0])
    total = gr_all[0]
    for a in range(1, ROW):
        total = total + gr_all[a]
    for h in range(heads):
        gg_ref[:, h * DIM:(h + 1) * DIM] = total[h:h + 1]
    few = 2 * (ROW - 1 + zs - 1) + heads * (ROW - 1 + rows - 1)
    for at_edge in (True, False):
        @pl.when((pos == 1) == at_edge)
        def _():
            sent(totals.at[0, pl.ds(0, few + HEAD_ROWS * at_edge)], small_s.at[0])
    @pl.when(core == 0)
    def _():
        sent(states, a2a_s.at[0])
        sent(pair, pair_s.at[0])

    @pl.when(core == 1)
    def _():
        sent(states.at[:, pl.ds(0, CHIPS - 1)], a2a_s.at[0])
        sent(prefixes.at[:, pl.ds(0, 5)], ret_s.at[0])
        sent(landed, pass_s.at[0])
        moved = jnp.minimum(row, 2) + jnp.minimum(rows - 1 - row, 2)
        for n in (2, 3, 4):
            @pl.when(moved == n)
            def _():
                sent(carried.at[pl.ds(0, n)], col_s.at[0])


def store(*refs):
    count = (len(refs) - 1) // 2
    for i in range(count):
        tall = refs[i].shape[0]
        for at in range(0, tall, 32):
            part = pl.ds(at, min(32, tall))
            pltpu.make_async_copy(
                refs[i].at[part], refs[count + i].at[part], refs[-1].at[i]
            ).start()
    for i in range(count):
        pltpu.make_async_copy(refs[i], refs[count + i], refs[-1].at[i]).wait()


def local(queries, key_rows, value_rows, segment_ids, decay_span, norm_gain, out_grad):
    rows = lax.axis_size("seq") // ROW
    zs = lax.axis_size("head")
    heads = decay_span.shape[0]
    width = heads * DIM
    far = pl.BlockSpec(memory_space=pl.ANY)
    near = pl.BlockSpec(memory_space=pltpu.VMEM)
    wide = pltpu.VMEM((BLOCK, width), BF16)
    pair = pltpu.VMEM((2, BLOCK, width), BF16)
    square = pltpu.VMEM((heads, DIM, DIM), F32)
    pieces = pltpu.VMEM((2, ROW, DIM, DIM), F32)
    per_head = pltpu.VMEM((2, heads, DIM, DIM), F32)
    dma = pltpu.SemaphoreType.DMA
    kept = pltpu.VMEM((1, width), F32)
    results = pl.pallas_call(
        functools.partial(kernel, rows, zs, heads),
        out_shape=(wide, wide, wide, kept),
        in_specs=[far] * 7,
        out_specs=(near,) * 4,
        scratch_shapes=[
            pair, pair,
            pltpu.VMEM((1, BLOCK), jnp.int32), pltpu.SMEM((heads,), F32), kept,
            pltpu.VMEM((2, DIM), F32),
            pltpu.VMEM((ROW, 2, DIM), F32),
            per_head,
            pieces,
            pltpu.VMEM((2, HEAD_ROWS + DIM, DIM), F32),
            pltpu.VMEM((4, HEAD_ROWS + DIM, DIM), F32),
            pieces,
            per_head,
            pltpu.VMEM((2, DIM), F32),
            pltpu.VMEM((zs, 2, DIM), F32),
            pltpu.VMEM((heads, DIM), F32),
            pltpu.VMEM((ROW, heads, DIM), F32),
            pltpu.VMEM((heads, DIM), F32),
            pltpu.VMEM((rows, heads, DIM), F32),
            square, square, square, square, square,
            pltpu.VMEM((heads, 2, DIM, DIM), BF16),
            dma((5,)),
            dma((1,)), dma((1,)),
            dma((1,)), dma((CHUNKS,)),
            dma((1,)), dma((2, CHUNKS)),
            dma((1,)), dma((CHIPS,)),
            dma((1,)), dma((1,)), dma((1,)),
            pltpu.SemaphoreType.REGULAR((2, 2)),
            pltpu.VMEM((HEAD_ROWS, DIM), F32), dma((1,)),
            square, square, square, square, square, square,
            pltpu.VMEM((heads, DIM, DIM), BF16),
            square, square, pltpu.VMEM((heads, DIM), F32),
            dma((1,)), dma((1,)), dma((1,)),
        ],
        compiler_params=pltpu.CompilerParams(collective_id=0, has_side_effects=True),
    )(
        queries, key_rows, value_rows, out_grad,
        segment_ids.reshape(1, BLOCK), decay_span, norm_gain.reshape(1, width),
    )
    out = jax.ShapeDtypeStruct((BLOCK, width), BF16)
    dq, dk, dv, gg = pl.pallas_call(
        store,
        out_shape=(out, out, out, jax.ShapeDtypeStruct((1, width), F32)),
        in_specs=[near] * 4,
        out_specs=(far,) * 4,
        scratch_shapes=[dma((4,))],
    )(*[pltpu.with_memory_space_constraint(r, pltpu.VMEM) for r in results])
    return dq, dk, dv, gg.reshape(width)


def solution(mesh):
    in_specs = (
        P("seq", "head"),
        P("seq", "head"),
        P("seq", "head"),
        P("seq"),
        P("head"),
        P("head"),
        P("seq", "head"),
    )
    out_specs = (P("seq", "head"), P("seq", "head"), P("seq", "head"), P("head"))
    return jax.shard_map(local, mesh=mesh, in_specs=in_specs, out_specs=out_specs, check_vma=False)
```
